128 devices in a mesh: lon: 16 (over z_hi, x, core), lat: 8 (over y, z_lo).
Axes of the slice: x: 4, y: 4, z: 4 (z_hi: 2, z_lo: 2; z = z_hi * 2 + z_lo), core: 2. Of those that a mesh axis runs over, the one named last changes fastest.
Arguments:
- state: float32 [75, 4, 128, 2048], P(None, None, 'lat', 'lon'), may hold values from -6 to 6
- depth_levels: int32 [128, 2048], P('lat', 'lon'), may hold values from 0 to 75, as said below
Outputs:
- new_state: float32 [75, 4, 128, 2048], P(None, None, 'lat', 'lon')
The draws below stay inside these ranges and needn't reach their ends.
Inputs may be any that keep to these rules, and one draw needn't show every extreme that they name: `depth_levels`: the number of wet levels of each column; land (0) grows more common eastward.
All inputs are finite; a program needn't handle non-finite values.
Results may differ from the reference program's by a relative error of at most 0.000059.
Values sent between devices are 32-bit elements; how exact they have to be, the bound alone decides.
A program may use at most 192 MiB of HBM per device.

```python
import jax
import jax.numpy as jnp
from jax import lax

NZ = 75
STEPS = 2
NX = 2048
NY = 128


def draw_depth_levels(key, part):
    level_key = jax.random.fold_in(key, 11)
    land_key = jax.random.fold_in(key, 23)
    levels = jax.random.randint(level_key, (NY, NX), 1, NZ + 1)
    columns = jnp.arange(NX, dtype=jnp.int32)[None, :]
    levels = jnp.where(columns == 0, NZ, levels)
    chance = jax.random.randint(land_key, (NY, NX), 0, 100)
    land = chance < 70 * columns // NX
    rows = jnp.arange(NY, dtype=jnp.int32)[:, None]
    land = jnp.logical_or(land, jnp.logical_and(rows == 0, columns == NX - 1))
    return jnp.where(land, 0, levels).astype(jnp.int32)


def block_scale(key, shape, shards, smallest, largest):
    level = 1.0
    for axis_at, blocks in shards:
        steps = jax.random.uniform(jax.random.fold_in(jax.random.fold_in(key, 6), axis_at), (blocks,), jnp.float32, smallest / len(shards), largest / len(shards))
        level = level * jnp.repeat(jnp.exp(steps), shape[axis_at] // blocks).reshape((-1,) + (1,) * (len(shape) - 1 - axis_at))
    return level


def centred(key, extent, deviation, bound, cuts=(), held_as=jnp.bfloat16):
    values = jax.random.normal(key, extent, jnp.float32) * deviation
    if len(cuts) > 0:
        values = block_scale(key, extent, cuts, -0.22, 0.18) * values
    return jnp.clip(values, min=-bound, max=bound).astype(held_as)


def setup_inputs(seed: int = 0) -> dict:
    seeds = jax.random.split(jax.random.key(seed), 3)
    state = centred(seeds[0], (NZ, 4, NY, NX), 1.0, 6.0, ((2, 8), (3, 16)), jnp.float32)
    depth_levels = draw_depth_levels(jax.random.fold_in(seeds[2], 71), 0)
    return dict(state=state, depth_levels=depth_levels)


ADVECTION = 0.25
SPREADING = 0.15
VERTICAL_MIX = 64.0


def wet_levels(depth_levels, levels):
    level_index = lax.broadcasted_iota(jnp.int32, (levels,) + depth_levels.shape, 0)
    return (level_index < depth_levels[None]).astype(jnp.float32)


def coriolis_rows(first_row, row_count, total_rows):
    row_index = first_row + jnp.arange(row_count, dtype=jnp.int32)
    mirrored = jnp.where(row_index >= total_rows, 2 * total_rows - 1 - row_index, row_index)
    return 0.1 + 0.4 * (mirrored.astype(jnp.float32) + 0.5) / total_rows


def sign_table(dtype):
    return jnp.array([1.0, 1.0, -1.0, -1.0, 1.0], dtype)


def tridiagonal_columns(provisional, wet_centre):
    zero_level = jnp.zeros_like(wet_centre[:1])
    below = jnp.concatenate([wet_centre[1:], zero_level], axis=0)
    above = jnp.concatenate([zero_level, wet_centre[:-1]], axis=0)
    lower_coef = VERTICAL_MIX * wet_centre * above
    upper_coef = VERTICAL_MIX * wet_centre * below
    diagonal = 1.0 + lower_coef + upper_coef

    def forward(carried, level_terms):
        prev_upper, prev_value = carried
        lower_k, diag_k, upper_k, value_k = level_terms
        denominator = diag_k - lower_k * prev_upper
        next_upper = upper_k / denominator
        next_value = (value_k - lower_k * prev_value) / denominator
        return (next_upper, next_value), (next_upper, next_value)

    start = (jnp.zeros_like(wet_centre[0]), jnp.zeros_like(provisional[0]))
    _, (upper_all, value_all) = lax.scan(forward, start, (lower_coef, diagonal, upper_coef, provisional))

    def backward(next_solution, level_terms):
        upper_k, value_k = level_terms
        solution = value_k - upper_k * next_solution
        return solution, solution

    _, solved = lax.scan(backward, jnp.zeros_like(provisional[0]), (upper_all, value_all), reverse=True)
    return solved


def advance(padded, coriolis):
    height = padded.shape[2] - 2
    breadth = padded.shape[3] - 2

    def shifted(array, row_off, col_off):
        return array[:, :, 1 + row_off:1 + row_off + height, 1 + col_off:1 + col_off + breadth]

    centre = shifted(padded, 0, 0)
    east_cell = shifted(padded, 0, 1)
    west_cell = shifted(padded, 0, -1)
    north_cell = shifted(padded, 1, 0)
    south_cell = shifted(padded, -1, 0)
    density = (-0.25 * padded[:, 0] + 0.75 * padded[:, 1]) * padded[:, 4]
    pressure = (0.2 * jnp.cumsum(density, axis=0))[:, None]
    grad_east = shifted(pressure, 0, 1)[:, 0] - shifted(pressure, 0, -1)[:, 0]
    grad_north = shifted(pressure, 1, 0)[:, 0] - shifted(pressure, -1, 0)[:, 0]
    values = centre[:, 0:4]
    wet_centre = centre[:, 4:5]
    flux_sum = (east_cell[:, 2:3] * east_cell[:, 0:4] - west_cell[:, 2:3] * west_cell[:, 0:4]
                + north_cell[:, 3:4] * north_cell[:, 0:4] - south_cell[:, 3:4] * south_cell[:, 0:4])
    spread = (east_cell[:, 4:5] * (east_cell[:, 0:4] - values) + west_cell[:, 4:5] * (west_cell[:, 0:4] - values)
              + north_cell[:, 4:5] * (north_cell[:, 0:4] - values) + south_cell[:, 4:5] * (south_cell[:, 0:4] - values))
    rotation = coriolis[1:1 + height][None, :, None]
    force_east = rotation * values[:, 3] - 0.5 * grad_east
    force_north = -rotation * values[:, 2] - 0.5 * grad_north
    forcing = jnp.concatenate([jnp.zeros_like(values[:, 0:2]), force_east[:, None], force_north[:, None]], axis=1)
    provisional = wet_centre * (values - ADVECTION * flux_sum + SPREADING * spread + forcing)
    return tridiagonal_columns(provisional, wet_centre)


def extend_global(full, halo_width):
    with_lon = jnp.concatenate([full[..., -halo_width:], full, full[..., :halo_width]], axis=3)
    total_rows = full.shape[2]
    folded = with_lon[:, :, total_rows - halo_width:, :][:, :, ::-1, ::-1] * sign_table(full.dtype)[None, :, None, None]
    southern = jnp.zeros_like(with_lon[:, :, :halo_width, :])
    return jnp.concatenate([southern, with_lon, folded], axis=2)


def reference(state, depth_levels):
    wet_field = wet_levels(depth_levels, state.shape[0]).astype(state.dtype)
    total_rows = state.shape[2]
    coriolis = coriolis_rows(-1, total_rows + 2, total_rows).astype(state.dtype)
    current = state
    for step_index in range(STEPS):
        full = jnp.concatenate([current, wet_field[:, None]], axis=1)
        current = advance(extend_global(full, 1), coriolis)
    return current
```

```python
import functools

import jax
import jax.numpy as jnp
from jax import lax
from jax.experimental import pallas as pl
from jax.experimental.pallas import tpu as pltpu
from jax.sharding import PartitionSpec as P

MESH = pl.DeviceIdType.MESH
F32 = jnp.float32
MIX = 64.0
ADV = 0.25
SPR = 0.15
PAD = 8


def kernel(nlon, nlat, nz, x, dep, out,
           st1, st2, vf, pb, ob, dpad, dm, tab,
           xc, g1, g2, pe, ve, xe, xe2, gd, dge, dce,
           cw, ce, hw, he,
           lsem, ssem, rsem, csem, crsem, dsem, bsem):
    rows = x.shape[2]
    half = rows // 8
    lon, lat = lax.axis_index("lon"), lax.axis_index("lat")
    west, east = (lax.rem(lon + nlon - 1, nlon), lat), (lax.rem(lon + 1, nlon), lat)
    north, south, mirror = (lon, lat + 1), (lon, lat - 1), (nlon - 1 - lon, lat)
    top, bottom = lat == nlat - 1, lat == 0
    lane = lax.broadcasted_iota(jnp.int32, (8, 128), 1)
    sub = lax.broadcasted_iota(jnp.int32, (8, 128), 0)
    lo = sub < 4

    barrier = pltpu.get_barrier_semaphore()

    def greet(device):
        pl.semaphore_signal(barrier, inc=1, device_id=device, device_id_type=MESH)

    greet(west)
    greet(east)

    @pl.when(jnp.logical_not(top))
    def _():
        greet(north)

    @pl.when(top)
    def _():
        greet(mirror)

    @pl.when(jnp.logical_not(bottom))
    def _():
        greet(south)

    def load(i, src, dst):
        return pltpu.make_async_copy(src, dst, lsem.at[i])

    loads = [
        load(0, x, st1.at[:, :, PAD:PAD + rows, :]),
        load(1, dep, dpad.at[PAD:PAD + rows, :]),
        load(2, x.at[:, :, 0, :], xc.at[:, 0:4, :]),
        load(3, x.at[:, :, rows - 1, :], xc.at[:, 4:8, :]),
    ]
    for one in loads:
        one.start()

    @pl.when(bottom)
    def _():
        pl.semaphore_wait(barrier, 3)

    @pl.when(jnp.logical_not(bottom))
    def _():
        pl.semaphore_wait(barrier, 4)

    def along_lat(step, south_row, north_row, ghost, slot):
        base = 4 * step

        def copy(src, dst, i, device):
            return pltpu.make_async_remote_copy(src, dst, ssem.at[base + i], rsem.at[base + i], device_id=device, device_id_type=MESH)

        up = copy(north_row, ghost(0), slot, north)
        over = copy(north_row, ghost(1), slot + 1, mirror)
        down = copy(south_row, ghost(1), slot + 1, south)
        return up, over, down

    def start_lat(up, over, down):
        @pl.when(jnp.logical_not(top))
        def _():
            up.start()

        @pl.when(top)
        def _():
            over.start()

        @pl.when(jnp.logical_not(bottom))
        def _():
            down.start()

    def recv_lat(up, over, down):
        @pl.when(jnp.logical_not(bottom))
        def _():
            up.wait_recv()

        down.wait_recv()

    def sent_lat(up, over, down):
        @pl.when(jnp.logical_not(top))
        def _():
            up.wait_send()

        @pl.when(top)
        def _():
            over.wait_send()

        @pl.when(jnp.logical_not(bottom))
        def _():
            down.wait_send()

    def ghost_in(buf):
        return lambda e: buf.at[:, 4 * e:4 * e + 4, :]

    lat_depth = along_lat(0, dep.at[0:1, :], dep.at[rows - 1:rows, :], lambda e: gd.at[e], 2)
    lat_1 = along_lat(0, x.at[:, :, 0, :], x.at[:, :, rows - 1, :], ghost_in(g1), 0)
    lat_2 = along_lat(1, xe.at[:, 0:4, :], xe.at[:, 4:8, :], ghost_in(g2), 0)
    start_lat(*lat_depth)
    start_lat(*lat_1)

    zero = jnp.zeros((8, 128), F32)

    @pl.when(bottom)
    def _():
        gd[0] = jnp.zeros_like(gd[0])

        def clear(k, c):
            g1[k, 0:4] = zero[0:4]
            g2[k, 0:4] = zero[0:4]
            return c

        lax.fori_loop(0, nz, clear, 0)

    def clear_pads(k, c):
        for ch in range(4):
            for st in (st1, st2):
                st[k, ch, 0:PAD, :] = zero
                st[k, ch, PAD + rows:PAD + rows + 8, :] = zero
        return c

    lax.fori_loop(0, nz, clear_pads, 0)

    def pivots(k, upper):
        pivot = jnp.where(k == 0, 1.0 + MIX, 1.0 + 2.0 * MIX - MIX * upper)
        inv = 1.0 / pivot
        tab[0, k] = inv
        tab[1, k] = 1.0 / (pivot - MIX)
        tab[2, k] = MIX * inv
        return MIX * inv

    lax.fori_loop(0, nz, pivots, zero)

    def pack(st, depth_too):
        def body(k, acc):
            acc = list(acc)
            here = lane == k
            for ch in range(4):
                for h in range(half):
                    v = st[k, ch, pl.ds(PAD + 8 * h, 8), :]
                    i = ch * half + h
                    acc[i] = jnp.where(here, pltpu.roll(v, k, 1), acc[i])
                    i += 4 * half
                    acc[i] = jnp.where(here, pltpu.roll(v, k + 1, 1), acc[i])
            return tuple(acc)

        acc = list(lax.fori_loop(0, nz, body, (zero,) * (8 * half)))
        if depth_too:
            for h in range(half):
                d = dpad[pl.ds(PAD + 8 * h, 8), :].astype(F32)
                acc[h] = jnp.where(lane == nz, pltpu.roll(d, nz, 1), acc[h])
                i = 4 * half + h
                acc[i] = jnp.where(lane == nz, pltpu.roll(d, nz + 1, 1), acc[i])
        return acc

    def lon_copies(step):
        def copy(src, dst, i, device):
            return pltpu.make_async_remote_copy(src, dst, csem.at[2 * step + i], crsem.at[2 * step + i], device_id=device, device_id_type=MESH)

        return [copy(cw.at[step], he.at[step], 0, west), copy(ce.at[step], hw.at[step], 1, east)]

    def send_lon(step, acc):
        for ch in range(4):
            for h in range(half):
                i = ch * half + h
                cw[step, ch, pl.ds(8 * h, 8), :] = acc[i]
                ce[step, ch, pl.ds(8 * h, 8), :] = acc[4 * half + i]
        copies = lon_copies(step)
        for one in copies:
            one.start()
        return copies

    loads[1].wait()
    dpad[0:PAD, :] = jnp.zeros((8, 128), jnp.int32)
    dpad[PAD + rows:PAD + rows + 8, :] = jnp.zeros((8, 128), jnp.int32)
    loads[0].wait()
    lon_1 = send_lon(0, pack(st1, True))

    def shifted(v, west_halo, east_halo, k):
        from_east = jnp.where(lane == 127, pltpu.roll(east_halo, 127 - k, 1), pltpu.roll(v, 127, 1))
        from_west = jnp.where(lane == 0, pltpu.roll(west_halo, lax.rem(128 - k, 128), 1), pltpu.roll(v, 1, 1))
        return from_east, from_west

    def depth_maps():
        for h in range(half):
            d = dpad[pl.ds(PAD + 8 * h, 8), :].astype(F32)
            e, w = shifted(d, hw[0, 0, pl.ds(8 * h, 8), :], he[0, 0, pl.ds(8 * h, 8), :], nz)
            at = pl.ds(8 * h, 8)
            dm[0, at, :] = d.astype(jnp.int32)
            dm[1, at, :] = e.astype(jnp.int32)
            dm[2, at, :] = w.astype(jnp.int32)
            dm[3, at, :] = dpad[pl.ds(PAD + 8 * h + 1, 8), :]
            dm[4, at, :] = dpad[pl.ds(PAD + 8 * h - 1, 8), :]

    total = F32(rows * nlat)

    def rotation(h):
        row = (sub + (8 * h + lat * rows)).astype(F32)
        return 0.1 + 0.4 * (row + 0.5) / total

    def main(st, step, dst, dst_row):
        def forward(k, carry):
            prev = list(carry[0:4 * half])
            grad_e = list(carry[4 * half:5 * half])
            grad_n = list(carry[5 * half:6 * half])
            inv_in, inv_low = tab[0, k], tab[1, k]
            for h in range(half):
                at = pl.ds(8 * h, 8)
                wet = []
                for i in range(5):
                    wet.append(k < dm[i, at, :])
                w15 = [jnp.where(m, F32(SPR), F32(0.0)) for m in wet[1:]]
                q, qe, qw, qn, qs = [], [], [], [], []
                for ch in range(4):
                    v = st[k, ch, pl.ds(PAD + 8 * h, 8), :]
                    e, w = shifted(v, hw[step, ch, at, :], he[step, ch, at, :], k)
                    q.append(v)
                    qe.append(e)
                    qw.append(w)
                    qn.append(st[k, ch, pl.ds(PAD + 8 * h + 1, 8), :])
                    qs.append(st[k, ch, pl.ds(PAD + 8 * h - 1, 8), :])
                a_e = w15[0] - ADV * qe[2]
                a_w = w15[1] + ADV * qw[2]
                a_n = w15[2] - ADV * qn[3]
                a_s = w15[3] + ADV * qs[3]
                centre = 1.0 - (w15[0] + w15[1]) - (w15[2] + w15[3])

                def dense(p, m):
                    return jnp.where(m, 0.75 * p[1] - 0.25 * p[0], 0.0)

                grad_e[h] = grad_e[h] + (dense(qe, wet[1]) - dense(qw, wet[2]))
                grad_n[h] = grad_n[h] + (dense(qn, wet[3]) - dense(qs, wet[4]))
                turn = rotation(h)
                low = (k + 1) == dm[0, at, :]
                inv = jnp.where(low, inv_low, inv_in)
                for ch in range(4):
                    p = (centre * q[ch] + a_e * qe[ch]) + (a_w * qw[ch] + a_n * qn[ch]) + a_s * qs[ch]
                    if ch == 2:
                        p = p + (turn * q[3] - 0.1 * grad_e[h])
                    if ch == 3:
                        p = p - (turn * q[2] + 0.1 * grad_n[h])
                    pb[k, ch, at, :] = p
                    i = ch * half + h
                    prev[i] = jnp.where(wet[0], (p - MIX * prev[i]) * inv, 0.0)
                    vf[k, ch, at, :] = prev[i]
            return tuple(prev + grad_e + grad_n)

        lax.fori_loop(0, nz, forward, (zero,) * (6 * half))

        copies = [pltpu.make_async_copy(pb.at[:, :, 0, :], pe.at[:, 0:4, :], dsem.at[0]),
                  pltpu.make_async_copy(pb.at[:, :, rows - 1, :], pe.at[:, 4:8, :], dsem.at[1])]
        for one in copies:
            one.start()

        def backward(j, carry):
            k = nz - 1 - j
            up = tab[2, k]
            new = []
            for ch in range(4):
                for h in range(half):
                    s = vf[k, ch, pl.ds(8 * h, 8), :] - up * carry[ch * half + h]
                    dst[k, ch, pl.ds(dst_row + 8 * h, 8), :] = s
                    new.append(s)
            return tuple(new)

        lax.fori_loop(0, nz, backward, (zero,) * (4 * half))
        for one in copies:
            one.wait()

    flip = jnp.logical_and(top, sub >= 4)
    index = jnp.where(flip, 127 - lane, lane)
    sign = jnp.where(jnp.logical_and(flip, lax.rem(sub, 4) >= 2), F32(-1.0), F32(1.0))
    slope = jnp.where(lo, F32(ADV), jnp.where(top, F32(ADV), F32(-ADV)))
    push = jnp.where(sub == 3, F32(0.1), jnp.where(sub == 7, F32(-0.1), F32(0.0)))

    def mirrored(v):
        return jnp.take_along_axis(v, index, axis=1)

    def edges(ghost, centre, solved):
        def both(k, c):
            return mirrored(jnp.where(lo, ghost[k, c:c + 1, :], ghost[k, c + 4:c + 5, :]))

        def forward(k, carry):
            prev, grad = carry
            g = mirrored(ghost[k])
            warm, salt, vel = both(k, 0), both(k, 1), both(k, 3)
            wet = k < dge[...]
            w15 = jnp.where(wet, F32(SPR), 0.0)
            grad = grad + push * jnp.where(wet, 0.75 * salt - 0.25 * warm, 0.0)
            p = pe[k] + ((w15 + slope * vel) * (sign * g) - w15 * centre[k]) + grad
            depth = dce[...]
            inv = jnp.where((k + 1) == depth, tab[1, k], tab[0, k])
            prev = jnp.where(k < depth, (p - MIX * prev) * inv, 0.0)
            ve[k] = prev
            return prev, grad

        lax.fori_loop(0, nz, forward, (zero, zero))

        def backward(j, s):
            k = nz - 1 - j
            s = ve[k] - tab[2, k] * s
            solved[k] = s
            return s

        lax.fori_loop(0, nz, backward, zero)

    for one in lon_1:
        one.wait_recv()
    depth_maps()
    main(st1, 0, st2, PAD)

    loads[2].wait()
    loads[3].wait()
    recv_lat(*lat_depth)
    dce[...] = jnp.where(lo, dm[0, 0:1, :], dm[0, rows - 1:rows, :])
    dge[...] = mirrored(jnp.where(lo, gd[0], gd[1]).astype(F32)).astype(jnp.int32)
    recv_lat(*lat_1)
    edges(g1, xc, xe)
    start_lat(*lat_2)
    patch = [pltpu.make_async_copy(xe.at[:, 0:4, :], st2.at[:, :, PAD, :], bsem.at[0]),
             pltpu.make_async_copy(xe.at[:, 4:8, :], st2.at[:, :, PAD + rows - 1, :], bsem.at[1])]
    for one in patch:
        one.start()
    for one in patch:
        one.wait()
    lon_2 = send_lon(1, pack(st2, False))
    for one in lon_2:
        one.wait_recv()
    main(st2, 1, ob, 0)
    whole = pltpu.make_async_copy(ob, out, bsem.at[2])
    whole.start()
    recv_lat(*lat_2)
    edges(g2, xe, xe2)
    whole.wait()
    last = [pltpu.make_async_copy(xe2.at[:, 0:4, :], out.at[:, :, 0, :], bsem.at[0]),
            pltpu.make_async_copy(xe2.at[:, 4:8, :], out.at[:, :, rows - 1, :], bsem.at[1])]
    for one in last:
        one.start()
    for one in lon_1 + lon_2:
        one.wait_send()
    sent_lat(*lat_depth)
    sent_lat(*lat_1)
    sent_lat(*lat_2)
    for one in last:
        one.wait()


def solution(mesh):
    nlon, nlat = mesh.shape["lon"], mesh.shape["lat"]

    def on_device(state, depth_levels):
        nz, _, rows, cols = state.shape
        edge = pltpu.VMEM((nz, 8, cols), F32)
        dma = pltpu.SemaphoreType.DMA
        return pl.pallas_call(
            functools.partial(kernel, nlon, nlat, nz),
            out_shape=jax.ShapeDtypeStruct(state.shape, F32),
            in_specs=[pl.BlockSpec(memory_space=pl.ANY)] * 2,
            out_specs=pl.BlockSpec(memory_space=pl.ANY),
            scratch_shapes=[
                pltpu.VMEM((nz, 4, rows + 16, cols), F32),
                pltpu.VMEM((nz, 4, rows + 16, cols), F32),
                pltpu.VMEM((nz, 4, rows, cols), F32),
                pltpu.VMEM((nz, 4, rows, cols), F32),
                pltpu.VMEM((nz, 4, rows, cols), F32),
                pltpu.VMEM((rows + 16, cols), jnp.int32),
                pltpu.VMEM((5, rows, cols), jnp.int32),
                pltpu.VMEM((3, nz, 8, cols), F32),
                edge, edge, edge, edge, edge, edge, edge,
                pltpu.VMEM((2, 1, cols), jnp.int32),
                pltpu.VMEM((8, cols), jnp.int32),
                pltpu.VMEM((8, cols), jnp.int32),
                pltpu.VMEM((2, 4, rows, cols), F32),
                pltpu.VMEM((2, 4, rows, cols), F32),
                pltpu.VMEM((2, 4, rows, cols), F32),
                pltpu.VMEM((2, 4, rows, cols), F32),
                dma((4,)), dma((8,)), dma((8,)), dma((4,)), dma((4,)), dma((2,)), dma((3,)),
            ],
            compiler_params=pltpu.CompilerParams(
                collective_id=0, has_side_effects=True, vmem_limit_bytes=48 << 20
            ),
        )(state, depth_levels)

    return jax.shard_map(
        on_device,
        mesh=mesh,
        in_specs=(P(None, None, "lat", "lon"), P("lat", "lon")),
        out_specs=P(None, None, "lat", "lon"),
        check_vma=False,
    )
```

```python
import functools

import jax
import jax.numpy as jnp
from jax import lax
from jax.experimental import pallas as pl
from jax.experimental.pallas import tpu as pltpu
from jax.sharding import PartitionSpec as P

MESH = pl.DeviceIdType.MESH
F32 = jnp.float32
MIX = 64.0
ADV = 0.25
SPR = 0.15
PAD = 8


def kernel(nlon, nlat, nz, x, dep, out,
           st1, st2, vf, pb, dpad, dm, tab,
           xc, g1, g2, pe, ve, xe, xe2, gd, dge, dce,
           cw, ce, hw, he,
           lsem, ssem, rsem, csem, crsem, dsem, bsem):
    rows = x.shape[2]
    half = rows // 8
    lon, lat = lax.axis_index("lon"), lax.axis_index("lat")
    west, east = (lax.rem(lon + nlon - 1, nlon), lat), (lax.rem(lon + 1, nlon), lat)
    north, south, mirror = (lon, lat + 1), (lon, lat - 1), (nlon - 1 - lon, lat)
    top, bottom = lat == nlat - 1, lat == 0
    lane = lax.broadcasted_iota(jnp.int32, (8, 128), 1)
    sub = lax.broadcasted_iota(jnp.int32, (8, 128), 0)
    lo = sub < 4

    barrier = pltpu.get_barrier_semaphore()

    def greet(device):
        pl.semaphore_signal(barrier, inc=1, device_id=device, device_id_type=MESH)

    greet(west)
    greet(east)

    @pl.when(jnp.logical_not(top))
    def _():
        greet(north)

    @pl.when(top)
    def _():
        greet(mirror)

    @pl.when(jnp.logical_not(bottom))
    def _():
        greet(south)

    def load(i, src, dst):
        return pltpu.make_async_copy(src, dst, lsem.at[i])

    loads = [
        load(0, x, st1.at[:, :, PAD:PAD + rows, :]),
        load(1, dep, dpad.at[PAD:PAD + rows, :]),
        load(2, x.at[:, :, 0, :], xc.at[:, 0:4, :]),
        load(3, x.at[:, :, rows - 1, :], xc.at[:, 4:8, :]),
    ]
    for one in loads:
        one.start()

    @pl.when(bottom)
    def _():
        pl.semaphore_wait(barrier, 3)

    @pl.when(jnp.logical_not(bottom))
    def _():
        pl.semaphore_wait(barrier, 4)

    def along_lat(step, south_row, north_row, ghost, slot):
        base = 4 * step

        def copy(src, dst, i, device):
            return pltpu.make_async_remote_copy(src, dst, ssem.at[base + i], rsem.at[base + i], device_id=device, device_id_type=MESH)

        up = copy(north_row, ghost(0), slot, north)
        over = copy(north_row, ghost(1), slot + 1, mirror)
        down = copy(south_row, ghost(1), slot + 1, south)
        return up, over, down

    def start_lat(up, over, down):
        @pl.when(jnp.logical_not(top))
        def _():
            up.start()

        @pl.when(top)
        def _():
            over.start()

        @pl.when(jnp.logical_not(bottom))
        def _():
            down.start()

    def recv_lat(up, over, down):
        @pl.when(jnp.logical_not(bottom))
        def _():
            up.wait_recv()

        down.wait_recv()

    def sent_lat(up, over, down):
        @pl.when(jnp.logical_not(top))
        def _():
            up.wait_send()

        @pl.when(top)
        def _():
            over.wait_send()

        @pl.when(jnp.logical_not(bottom))
        def _():
            down.wait_send()

    def ghost_in(buf):
        return lambda e: buf.at[:, 4 * e:4 * e + 4, :]

    lat_depth = along_lat(0, dep.at[0:1, :], dep.at[rows - 1:rows, :], lambda e: gd.at[e], 2)
    lat_1 = along_lat(0, x.at[:, :, 0, :], x.at[:, :, rows - 1, :], ghost_in(g1), 0)
    lat_2 = along_lat(1, xe.at[:, 0:4, :], xe.at[:, 4:8, :], ghost_in(g2), 0)
    start_lat(*lat_depth)
    start_lat(*lat_1)

    zero = jnp.zeros((8, 128), F32)

    @pl.when(bottom)
    def _():
        gd[0] = jnp.zeros_like(gd[0])

        def clear(k, c):
            g1[k, 0:4] = zero[0:4]
            g2[k, 0:4] = zero[0:4]
            return c

        lax.fori_loop(0, nz, clear, 0, unroll=5)

    def clear_pads(k, c):
        for ch in range(4):
            for st in (st1, st2):
                st[k, ch, 0:PAD, :] = zero
                st[k, ch, PAD + rows:PAD + rows + 8, :] = zero
        return c

    lax.fori_loop(0, nz, clear_pads, 0, unroll=5)

    def pivots(k, upper):
        pivot = jnp.where(k == 0, 1.0 + MIX, 1.0 + 2.0 * MIX - MIX * upper)
        inv = 1.0 / pivot
        tab[0, k] = inv
        tab[1, k] = 1.0 / (pivot - MIX)
        tab[2, k] = MIX * inv
        return MIX * inv

    lax.fori_loop(0, nz, pivots, zero, unroll=5)

    def pack(st, depth_too):
        def body(k, acc):
            acc = list(acc)
            here = lane == k
            for ch in range(4):
                for h in range(half):
                    v = st[k, ch, pl.ds(PAD + 8 * h, 8), :]
                    i = ch * half + h
                    acc[i] = jnp.where(here, pltpu.roll(v, k, 1), acc[i])
                    i += 4 * half
                    acc[i] = jnp.where(here, pltpu.roll(v, k + 1, 1), acc[i])
            return tuple(acc)

        acc = list(lax.fori_loop(0, nz, body, (zero,) * (8 * half), unroll=15))
        if depth_too:
            for h in range(half):
                d = dpad[pl.ds(PAD + 8 * h, 8), :].astype(F32)
                acc[h] = jnp.where(lane == nz, pltpu.roll(d, nz, 1), acc[h])
                i = 4 * half + h
                acc[i] = jnp.where(lane == nz, pltpu.roll(d, nz + 1, 1), acc[i])
        return acc

    def lon_copies(step):
        def copy(src, dst, i, device):
            return pltpu.make_async_remote_copy(src, dst, csem.at[2 * step + i], crsem.at[2 * step + i], device_id=device, device_id_type=MESH)

        return [copy(cw.at[step], he.at[step], 0, west), copy(ce.at[step], hw.at[step], 1, east)]

    def send_lon(step, acc):
        for ch in range(4):
            for h in range(half):
                i = ch * half + h
                cw[step, ch, pl.ds(8 * h, 8), :] = acc[i]
                ce[step, ch, pl.ds(8 * h, 8), :] = acc[4 * half + i]
        copies = lon_copies(step)
        for one in copies:
            one.start()
        return copies

    loads[1].wait()
    dpad[0:PAD, :] = jnp.zeros((8, 128), jnp.int32)
    dpad[PAD + rows:PAD + rows + 8, :] = jnp.zeros((8, 128), jnp.int32)
    loads[0].wait()
    lon_1 = send_lon(0, pack(st1, True))

    def shifted(v, west_halo, east_halo, k):
        from_east = jnp.where(lane == 127, pltpu.roll(east_halo, 127 - k, 1), pltpu.roll(v, 127, 1))
        from_west = jnp.where(lane == 0, pltpu.roll(west_halo, lax.rem(128 - k, 128), 1), pltpu.roll(v, 1, 1))
        return from_east, from_west

    def depth_maps():
        for h in range(half):
            d = dpad[pl.ds(PAD + 8 * h, 8), :].astype(F32)
            e, w = shifted(d, hw[0, 0, pl.ds(8 * h, 8), :], he[0, 0, pl.ds(8 * h, 8), :], nz)
            at = pl.ds(8 * h, 8)
            dm[0, at, :] = d.astype(jnp.int32)
            dm[1, at, :] = e.astype(jnp.int32)
            dm[2, at, :] = w.astype(jnp.int32)
            dm[3, at, :] = dpad[pl.ds(PAD + 8 * h + 1, 8), :]
            dm[4, at, :] = dpad[pl.ds(PAD + 8 * h - 1, 8), :]

    total = F32(rows * nlat)

    def rotation(h):
        row = (sub + (8 * h + lat * rows)).astype(F32)
        return 0.1 + 0.4 * (row + 0.5) / total

    def main(st, step, dst, dst_row):
        def forward(k, carry):
            prev = list(carry[0:4 * half])
            grad_e = list(carry[4 * half:5 * half])
            grad_n = list(carry[5 * half:6 * half])
            inv_in, inv_low = tab[0, k], tab[1, k]
            for h in range(half):
                at = pl.ds(8 * h, 8)
                wet = []
                for i in range(5):
                    wet.append(k < dm[i, at, :])
                w15 = [jnp.where(m, F32(SPR), F32(0.0)) for m in wet[1:]]
                q, qe, qw, qn, qs = [], [], [], [], []
                for ch in range(4):
                    v = st[k, ch, pl.ds(PAD + 8 * h, 8), :]
                    e, w = shifted(v, hw[step, ch, at, :], he[step, ch, at, :], k)
                    q.append(v)
                    qe.append(e)
                    qw.append(w)
                    qn.append(st[k, ch, pl.ds(PAD + 8 * h + 1, 8), :])
                    qs.append(st[k, ch, pl.ds(PAD + 8 * h - 1, 8), :])
                a_e = w15[0] - ADV * qe[2]
                a_w = w15[1] + ADV * qw[2]
                a_n = w15[2] - ADV * qn[3]
                a_s = w15[3] + ADV * qs[3]
                centre = 1.0 - (w15[0] + w15[1]) - (w15[2] + w15[3])

                def dense(p, m):
                    return jnp.where(m, 0.75 * p[1] - 0.25 * p[0], 0.0)

                grad_e[h] = grad_e[h] + (dense(qe, wet[1]) - dense(qw, wet[2]))
                grad_n[h] = grad_n[h] + (dense(qn, wet[3]) - dense(qs, wet[4]))
                turn = rotation(h)
                low = (k + 1) == dm[0, at, :]
                inv = jnp.where(low, inv_low, inv_in)
                for ch in range(4):
                    p = (centre * q[ch] + a_e * qe[ch]) + (a_w * qw[ch] + a_n * qn[ch]) + a_s * qs[ch]
                    if ch == 2:
                        p = p + (turn * q[3] - 0.1 * grad_e[h])
                    if ch == 3:
                        p = p - (turn * q[2] + 0.1 * grad_n[h])
                    pb[k, ch, at, :] = p
                    i = ch * half + h
                    prev[i] = jnp.where(wet[0], (p - MIX * prev[i]) * inv, 0.0)
                    vf[k, ch, at, :] = prev[i]
            return tuple(prev + grad_e + grad_n)

        lax.fori_loop(0, nz, forward, (zero,) * (6 * half), unroll=5)

        copies = [pltpu.make_async_copy(pb.at[:, :, 0, :], pe.at[:, 0:4, :], dsem.at[0]),
                  pltpu.make_async_copy(pb.at[:, :, rows - 1, :], pe.at[:, 4:8, :], dsem.at[1])]
        for one in copies:
            one.start()

        def backward(j, carry):
            k = nz - 1 - j
            up = tab[2, k]
            new = []
            for ch in range(4):
                for h in range(half):
                    s = vf[k, ch, pl.ds(8 * h, 8), :] - up * carry[ch * half + h]
                    dst[k, ch, pl.ds(dst_row + 8 * h, 8), :] = s
                    new.append(s)
            return tuple(new)

        lax.fori_loop(0, nz, backward, (zero,) * (4 * half), unroll=15)
        for one in copies:
            one.wait()

    flip = jnp.logical_and(top, sub >= 4)
    index = jnp.where(flip, 127 - lane, lane)
    sign = jnp.where(jnp.logical_and(flip, lax.rem(sub, 4) >= 2), F32(-1.0), F32(1.0))
    slope = jnp.where(lo, F32(ADV), jnp.where(top, F32(ADV), F32(-ADV)))
    push = jnp.where(sub == 3, F32(0.1), jnp.where(sub == 7, F32(-0.1), F32(0.0)))

    def mirrored(v):
        return jnp.take_along_axis(v, index, axis=1)

    def edges(ghost, centre, solved):
        def both(k, c):
            return mirrored(jnp.where(lo, ghost[k, c:c + 1, :], ghost[k, c + 4:c + 5, :]))

        def forward(k, carry):
            prev, grad = carry
            g = mirrored(ghost[k])
            warm, salt, vel = both(k, 0), both(k, 1), both(k, 3)
            wet = k < dge[...]
            w15 = jnp.where(wet, F32(SPR), 0.0)
            grad = grad + push * jnp.where(wet, 0.75 * salt - 0.25 * warm, 0.0)
            p = pe[k] + ((w15 + slope * vel) * (sign * g) - w15 * centre[k]) + grad
            depth = dce[...]
            inv = jnp.where((k + 1) == depth, tab[1, k], tab[0, k])
            prev = jnp.where(k < depth, (p - MIX * prev) * inv, 0.0)
            ve[k] = prev
            return prev, grad

        lax.fori_loop(0, nz, forward, (zero, zero), unroll=25)

        def backward(j, s):
            k = nz - 1 - j
            s = ve[k] - tab[2, k] * s
            solved[k] = s
            return s

        lax.fori_loop(0, nz, backward, zero, unroll=25)

    for one in lon_1:
        one.wait_recv()
    depth_maps()
    main(st1, 0, st2, PAD)

    loads[2].wait()
    loads[3].wait()
    recv_lat(*lat_depth)
    dce[...] = jnp.where(lo, dm[0, 0:1, :], dm[0, rows - 1:rows, :])
    dge[...] = mirrored(jnp.where(lo, gd[0], gd[1]).astype(F32)).astype(jnp.int32)
    recv_lat(*lat_1)
    edges(g1, xc, xe)
    start_lat(*lat_2)
    patch = [pltpu.make_async_copy(xe.at[:, 0:4, :], st2.at[:, :, PAD, :], bsem.at[0]),
             pltpu.make_async_copy(xe.at[:, 4:8, :], st2.at[:, :, PAD + rows - 1, :], bsem.at[1])]
    for one in patch:
        one.start()
    for one in patch:
        one.wait()
    lon_2 = send_lon(1, pack(st2, False))
    for one in lon_2:
        one.wait_recv()
    main(st2, 1, out, 0)
    recv_lat(*lat_2)
    edges(g2, xe, xe2)
    last = [pltpu.make_async_copy(xe2.at[:, 0:4, :], out.at[:, :, 0, :], bsem.at[0]),
            pltpu.make_async_copy(xe2.at[:, 4:8, :], out.at[:, :, rows - 1, :], bsem.at[1])]
    for one in last:
        one.start()
    for one in lon_1 + lon_2:
        one.wait_send()
    sent_lat(*lat_depth)
    sent_lat(*lat_1)
    sent_lat(*lat_2)
    for one in last:
        one.wait()


def solution(mesh):
    nlon, nlat = mesh.shape["lon"], mesh.shape["lat"]

    def on_device(state, depth_levels):
        nz, _, rows, cols = state.shape
        edge = pltpu.VMEM((nz, 8, cols), F32)
        dma = pltpu.SemaphoreType.DMA
        return pl.pallas_call(
            functools.partial(kernel, nlon, nlat, nz),
            out_shape=jax.ShapeDtypeStruct(state.shape, F32),
            in_specs=[pl.BlockSpec(memory_space=pltpu.HBM)] * 2,
            out_specs=pl.BlockSpec(memory_space=pltpu.VMEM),
            scratch_shapes=[
                pltpu.VMEM((nz, 4, rows + 16, cols), F32),
                pltpu.VMEM((nz, 4, rows + 16, cols), F32),
                pltpu.VMEM((nz, 4, rows, cols), F32),
                pltpu.VMEM((nz, 4, rows, cols), F32),
                pltpu.VMEM((rows + 16, cols), jnp.int32),
                pltpu.VMEM((5, rows, cols), jnp.int32),
                pltpu.VMEM((3, nz, 8, cols), F32),
                edge, edge, edge, edge, edge, edge, edge,
                pltpu.VMEM((2, 1, cols), jnp.int32),
                pltpu.VMEM((8, cols), jnp.int32),
                pltpu.VMEM((8, cols), jnp.int32),
                pltpu.VMEM((2, 4, rows, cols), F32),
                pltpu.VMEM((2, 4, rows, cols), F32),
                pltpu.VMEM((2, 4, rows, cols), F32),
                pltpu.VMEM((2, 4, rows, cols), F32),
                dma((4,)), dma((8,)), dma((8,)), dma((4,)), dma((4,)), dma((2,)), dma((2,)),
            ],
            compiler_params=pltpu.CompilerParams(
                collective_id=0, has_side_effects=True, vmem_limit_bytes=48 << 20
            ),
        )(state, depth_levels)

    return jax.shard_map(
        on_device,
        mesh=mesh,
        in_specs=(P(None, None, "lat", "lon"), P("lat", "lon")),
        out_specs=P(None, None, "lat", "lon"),
        check_vma=False,
    )
```

```python
import functools

import jax
import jax.numpy as jnp
from jax import lax
from jax.experimental import pallas as pl
from jax.experimental.pallas import tpu as pltpu
from jax.sharding import PartitionSpec as P

MESH = pl.DeviceIdType.MESH
F32 = jnp.float32
MIX = 64.0
ADV = 0.25
SPR = 0.15
PAD = 8


def kernel(nlon, nlat, nz, x, dep, out,
           st1, st2, vf, pb, dpad, dm, tab,
           xc, g1, g2, pe, ve, xe, xe2, h1, h2, hd, gd, dge, dce,
           cw, ce, hw, he, ca,
           lsem, ssem, rsem, csem, crsem, dsem, bsem):
    rows = x.shape[2]
    half = rows // 8
    lon, lat = lax.axis_index("lon"), lax.axis_index("lat")
    west, east = (lax.rem(lon + nlon - 1, nlon), lat), (lax.rem(lon + 1, nlon), lat)
    north, south = (lon, lat + 1), (lon, lat - 1)
    top, near, bottom = lat == nlat - 1, lat == nlat - 2, lat == 0
    over_south, over_north = (nlon - 1 - lon, lat - 1), (nlon - 1 - lon, lat + 1)
    lane = lax.broadcasted_iota(jnp.int32, (8, 128), 1)
    sub = lax.broadcasted_iota(jnp.int32, (8, 128), 0)
    lo = sub < 4

    barrier = pltpu.get_barrier_semaphore()

    def greet(device):
        pl.semaphore_signal(barrier, inc=1, device_id=device, device_id_type=MESH)

    greet(west)
    greet(east)

    @pl.when(jnp.logical_not(top))
    def _():
        greet(north)

    @pl.when(top)
    def _():
        greet(over_south)

    @pl.when(near)
    def _():
        greet(over_north)

    @pl.when(jnp.logical_not(bottom))
    def _():
        greet(south)

    def load(i, src, dst):
        return pltpu.make_async_copy(src, dst, lsem.at[i])

    loads = [
        load(0, x, st1.at[:, :, PAD:PAD + rows, :]),
        load(1, dep, dpad.at[PAD:PAD + rows, :]),
        load(2, x.at[:, :, 0, :], xc.at[:, 0:4, :]),
        load(3, x.at[:, :, rows - 1, :], xc.at[:, 4:8, :]),
    ]
    for one in loads:
        one.start()

    @pl.when(bottom)
    def _():
        pl.semaphore_wait(barrier, 3)

    @pl.when(near)
    def _():
        pl.semaphore_wait(barrier, 5)

    @pl.when(jnp.logical_not(jnp.logical_or(bottom, near)))
    def _():
        pl.semaphore_wait(barrier, 4)

    def along_lat(base, south_row, north_row, ghost, held, parts):
        def copy(src, dst, i, device):
            return pltpu.make_async_remote_copy(src, dst, ssem.at[i], rsem.at[i], device_id=device, device_id_type=MESH)

        up = copy(north_row, ghost(0), base, north)
        down = copy(south_row, ghost(1), base + 1, south)
        over, on = [], []
        for j, (at, size) in enumerate(parts):
            part = pl.ds(at, size)
            over.append(copy(north_row.at[part], held.at[part], base + 2 + 2 * j, over_south))
            on.append(copy(held.at[part], ghost(1).at[part], base + 3 + 2 * j, north))
        return up, down, over, on

    def start_lat(up, down, over, on):
        @pl.when(top)
        def _():
            for one in over:
                one.start()

        @pl.when(jnp.logical_not(top))
        def _():
            up.start()

        @pl.when(jnp.logical_not(bottom))
        def _():
            down.start()

    def relay(lats, j):
        @pl.when(near)
        def _():
            lats[2][j].wait_recv()
            lats[3][j].start()

    def recv_lat(up, down, over, on):
        @pl.when(jnp.logical_not(bottom))
        def _():
            up.wait_recv()

        @pl.when(jnp.logical_not(top))
        def _():
            down.wait_recv()

        @pl.when(top)
        def _():
            for one in on:
                one.wait_recv()

    def sent_lat(up, down, over, on):
        @pl.when(jnp.logical_not(top))
        def _():
            up.wait_send()

        @pl.when(top)
        def _():
            for one in over:
                one.wait_send()

        @pl.when(near)
        def _():
            for one in on:
                one.wait_send()

        @pl.when(jnp.logical_not(bottom))
        def _():
            down.wait_send()

    def ghost_in(buf):
        return lambda e: buf.at[:, 4 * e:4 * e + 4, :]

    third = nz // 3
    parts = [(0, third), (third, third), (2 * third, nz - 2 * third)]
    lat_depth = along_lat(0, dep.at[0:1, :], dep.at[rows - 1:rows, :], lambda e: gd.at[e], hd, [(0, 1)])
    lat_1 = along_lat(4, x.at[:, :, 0, :], x.at[:, :, rows - 1, :], ghost_in(g1), h1, parts)
    lat_2 = along_lat(12, xe.at[:, 0:4, :], xe.at[:, 4:8, :], ghost_in(g2), h2, parts)
    start_lat(*lat_depth)
    start_lat(*lat_1)

    zero = jnp.zeros((8, 128), F32)

    @pl.when(bottom)
    def _():
        gd[0] = jnp.zeros_like(gd[0])

        def clear(k, c):
            g1[k, 0:4] = zero[0:4]
            g2[k, 0:4] = zero[0:4]
            return c

        lax.fori_loop(0, nz, clear, 0, unroll=5)

    def clear_pads(k, c):
        for ch in range(4):
            for st in (st1, st2):
                st[k, ch, 0:PAD, :] = zero
                st[k, ch, PAD + rows:PAD + rows + 8, :] = zero
        return c

    lax.fori_loop(0, nz, clear_pads, 0, unroll=5)

    def pack(st, depth_too):
        def body(k, acc):
            acc = list(acc)
            here = lane == k
            for ch in range(4):
                for h in range(half):
                    v = st[k, ch, pl.ds(PAD + 8 * h, 8), :]
                    i = ch * half + h
                    acc[i] = jnp.where(here, pltpu.roll(v, k, 1), acc[i])
                    i += 4 * half
                    acc[i] = jnp.where(here, pltpu.roll(v, k + 1, 1), acc[i])
            return tuple(acc)

        acc = list(lax.fori_loop(0, nz, body, (zero,) * (8 * half), unroll=15))
        if depth_too:
            for h in range(half):
                d = dpad[pl.ds(PAD + 8 * h, 8), :].astype(F32)
                acc[h] = jnp.where(lane == nz, pltpu.roll(d, nz, 1), acc[h])
                i = 4 * half + h
                acc[i] = jnp.where(lane == nz, pltpu.roll(d, nz + 1, 1), acc[i])
        return acc

    def lon_copies(step):
        def copy(src, dst, i, device):
            return pltpu.make_async_remote_copy(src, dst, csem.at[2 * step + i], crsem.at[2 * step + i], device_id=device, device_id_type=MESH)

        return [copy(cw.at[step], he.at[step], 0, west), copy(ce.at[step], hw.at[step], 1, east)]

    def send_lon(step, acc):
        for ch in range(4):
            for h in range(half):
                i = ch * half + h
                cw[step, ch, pl.ds(8 * h, 8), :] = acc[i]
                ce[step, ch, pl.ds(8 * h, 8), :] = acc[4 * half + i]
        copies = lon_copies(step)
        for one in copies:
            one.start()
        return copies

    loads[1].wait()
    dpad[0:PAD, :] = jnp.zeros((8, 128), jnp.int32)
    dpad[PAD + rows:PAD + rows + 8, :] = jnp.zeros((8, 128), jnp.int32)
    loads[0].wait()
    lon_1 = send_lon(0, pack(st1, True))

    first, final = lane == 0, lane == 127

    def depth_maps():
        for h in range(half):
            at = pl.ds(8 * h, 8)
            d = dpad[pl.ds(PAD + 8 * h, 8), :]
            dm[0, at, :] = d
            dm[1, at, :] = jnp.where(final, 0, pltpu.roll(d, 127, 1))
            dm[2, at, :] = jnp.where(first, 0, pltpu.roll(d, 1, 1))
            dm[3, at, :] = dpad[pl.ds(PAD + 8 * h + 1, 8), :]
            dm[4, at, :] = dpad[pl.ds(PAD + 8 * h - 1, 8), :]

    total = F32(rows * nlat)

    def rotation(h):
        row = (sub + (8 * h + lat * rows)).astype(F32)
        return 0.1 + 0.4 * (row + 0.5) / total

    def dense(warm, salt, wet):
        return jnp.where(wet, 0.75 * salt - 0.25 * warm, 0.0)

    def stencil(st, make_table):
        def body(k, carry):
            grad_e = list(carry[0:half])
            grad_n = list(carry[half:2 * half])
            upper = carry[2 * half]
            if make_table:
                pivot = jnp.where(k == 0, 1.0 + MIX, 1.0 + 2.0 * MIX - MIX * upper)
                inv = 1.0 / pivot
                upper = MIX * inv
                tab[0, k] = inv
                tab[1, k] = 1.0 / (pivot - MIX)
                tab[2, k] = upper
            for h in range(half):
                at = pl.ds(8 * h, 8)
                wet = [None] + [k < dm[i, at, :] for i in range(1, 5)]
                w15 = [jnp.where(m, F32(SPR), F32(0.0)) for m in wet[1:]]
                q = [st[k, ch, pl.ds(PAD + 8 * h, 8), :] for ch in range(4)]
                qe = [pltpu.roll(v, 127, 1) for v in q]
                qw = [pltpu.roll(v, 1, 1) for v in q]
                qn = [st[k, ch, pl.ds(PAD + 8 * h + 1, 8), :] for ch in range(4)]
                qs = [st[k, ch, pl.ds(PAD + 8 * h - 1, 8), :] for ch in range(4)]
                a_e = jnp.where(final, 0.0, w15[0] - ADV * qe[2])
                a_w = jnp.where(first, 0.0, w15[1] + ADV * qw[2])
                a_n = w15[2] - ADV * qn[3]
                a_s = w15[3] + ADV * qs[3]
                centre = 1.0 - (w15[0] + w15[1]) - (w15[2] + w15[3])
                grad_e[h] = grad_e[h] + (dense(qe[0], qe[1], wet[1]) - dense(qw[0], qw[1], wet[2]))
                grad_n[h] = grad_n[h] + (dense(qn[0], qn[1], wet[3]) - dense(qs[0], qs[1], wet[4]))
                turn = rotation(h)
                for ch in range(4):
                    p = (centre * q[ch] + a_e * qe[ch]) + (a_w * qw[ch] + a_n * qn[ch]) + a_s * qs[ch]
                    if ch == 2:
                        p = p + (turn * q[3] - 0.1 * grad_e[h])
                    if ch == 3:
                        p = p - (turn * q[2] + 0.1 * grad_n[h])
                    pb[k, ch, at, :] = p
            return tuple(grad_e + grad_n + [upper])

        lax.fori_loop(0, nz, body, (zero,) * (2 * half + 1), unroll=5)

    def columns(step):
        for h in range(half):
            at = pl.ds(8 * h, 8)
            adds = []
            for halo, own, way in ((hw, cw, 1.0), (he, ce, -1.0)):
                deep = jnp.broadcast_to(halo[0, 0, at, nz:nz + 1], (8, 128)).astype(jnp.int32)
                wet = lane < deep
                w15 = jnp.where(wet, F32(SPR), F32(0.0))
                q = [halo[step, ch, at, :] for ch in range(4)]
                coef = w15 + (way * ADV) * q[2]
                push = dense(q[0], q[1], wet)
                shift = 1
                while shift < nz:
                    push = push + jnp.where(lane >= shift, pltpu.roll(push, shift, 1), 0.0)
                    shift *= 2
                add = [coef * q[ch] - w15 * own[step, ch, at, :] for ch in range(4)]
                add[2] = add[2] + (way * 0.1) * push
                adds.append(add)
            even = lax.rem(lane, 2) == 0
            for ch in range(4):
                w, e = adds[0][ch], pltpu.roll(adds[1][ch], 127, 1)
                ca[0, ch, at, :] = jnp.where(even, w, e)
                ca[1, ch, at, :] = jnp.where(even, e, w)

    outer = jnp.logical_or(first, final)

    def inverse(k, depth):
        inv = jnp.where((k + 1) == depth, tab[1, k], tab[0, k])
        return jnp.where(k < depth, inv, 0.0)

    def sweeps(dst, dst_row, lats):
        def forward(k, carry):
            new = list(carry)
            back = lax.rem(128 - k, 128)
            odd = lax.rem(k, 2)
            for h in range(half):
                at = pl.ds(8 * h, 8)
                inv = inverse(k, dm[0, at, :])
                low = MIX * inv
                for ch in range(4):
                    p = pb[k, ch, at, :] + jnp.where(outer, pltpu.roll(ca[odd, ch, at, :], back, 1), 0.0)
                    pb[k, ch, at, :] = p
                    i = ch * half + h
                    new[i] = p * inv - low * new[i]
                    vf[k, ch, at, :] = new[i]
            return tuple(new)

        carry = (zero,) * (4 * half)
        for j, (at, size) in enumerate(parts):
            carry = lax.fori_loop(at, at + size, forward, carry, unroll=5)
            if j == 0:
                relay(lats, 2)

        copies = [pltpu.make_async_copy(pb.at[:, :, 0, :], pe.at[:, 0:4, :], dsem.at[0]),
                  pltpu.make_async_copy(pb.at[:, :, rows - 1, :], pe.at[:, 4:8, :], dsem.at[1])]
        for one in copies:
            one.start()

        def backward(j, carry):
            k = nz - 1 - j
            up = tab[2, k]
            new = []
            for ch in range(4):
                for h in range(half):
                    s = vf[k, ch, pl.ds(8 * h, 8), :] - up * carry[ch * half + h]
                    dst[k, ch, pl.ds(dst_row + 8 * h, 8), :] = s
                    new.append(s)
            return tuple(new)

        lax.fori_loop(0, nz, backward, (zero,) * (4 * half), unroll=15)
        for one in copies:
            one.wait()

    flip = jnp.logical_and(top, sub >= 4)
    index = jnp.where(flip, 127 - lane, lane)
    sign = jnp.where(jnp.logical_and(flip, lax.rem(sub, 4) >= 2), F32(-1.0), F32(1.0))
    slope = jnp.where(lo, F32(ADV), jnp.where(top, F32(ADV), F32(-ADV)))
    push = jnp.where(sub == 3, F32(0.1), jnp.where(sub == 7, F32(-0.1), F32(0.0)))

    def mirrored(v):
        return jnp.take_along_axis(v, index, axis=1)

    def edges(ghost, centre, solved):
        def both(k, c):
            return mirrored(jnp.where(lo, ghost[k, c:c + 1, :], ghost[k, c + 4:c + 5, :]))

        def forward(k, carry):
            prev, grad = carry
            g = mirrored(ghost[k])
            warm, salt, vel = both(k, 0), both(k, 1), both(k, 3)
            wet = k < dge[...]
            w15 = jnp.where(wet, F32(SPR), 0.0)
            grad = grad + push * jnp.where(wet, 0.75 * salt - 0.25 * warm, 0.0)
            p = pe[k] + ((w15 + slope * vel) * (sign * g) - w15 * centre[k]) + grad
            inv = inverse(k, dce[...])
            prev = p * inv - (MIX * inv) * prev
            ve[k] = prev
            return prev, grad

        lax.fori_loop(0, nz, forward, (zero, zero), unroll=25)

        def backward(j, s):
            k = nz - 1 - j
            s = ve[k] - tab[2, k] * s
            solved[k] = s
            return s

        lax.fori_loop(0, nz, backward, zero, unroll=25)

    depth_maps()
    relay(lat_depth, 0)
    stencil(st1, True)
    relay(lat_1, 0)
    for one in lon_1:
        one.wait_recv()
    columns(0)
    relay(lat_1, 1)
    sweeps(st2, PAD, lat_1)

    loads[2].wait()
    loads[3].wait()
    recv_lat(*lat_depth)
    dce[...] = jnp.where(lo, dm[0, 0:1, :], dm[0, rows - 1:rows, :])
    dge[...] = mirrored(jnp.where(lo, gd[0], gd[1]).astype(F32)).astype(jnp.int32)
    recv_lat(*lat_1)
    edges(g1, xc, xe)
    start_lat(*lat_2)
    patch = [pltpu.make_async_copy(xe.at[:, 0:4, :], st2.at[:, :, PAD, :], bsem.at[0]),
             pltpu.make_async_copy(xe.at[:, 4:8, :], st2.at[:, :, PAD + rows - 1, :], bsem.at[1])]
    for one in patch:
        one.start()
    for one in patch:
        one.wait()
    lon_2 = send_lon(1, pack(st2, False))
    stencil(st2, False)
    relay(lat_2, 0)
    for one in lon_2:
        one.wait_recv()
    columns(1)
    relay(lat_2, 1)
    sweeps(out, 0, lat_2)
    recv_lat(*lat_2)
    edges(g2, xe, xe2)
    last = [pltpu.make_async_copy(xe2.at[:, 0:4, :], out.at[:, :, 0, :], bsem.at[0]),
            pltpu.make_async_copy(xe2.at[:, 4:8, :], out.at[:, :, rows - 1, :], bsem.at[1])]
    for one in last:
        one.start()
    for one in lon_1 + lon_2:
        one.wait_send()
    sent_lat(*lat_depth)
    sent_lat(*lat_1)
    sent_lat(*lat_2)
    for one in last:
        one.wait()


def solution(mesh):
    nlon, nlat = mesh.shape["lon"], mesh.shape["lat"]

    def on_device(state, depth_levels):
        nz, _, rows, cols = state.shape
        edge = pltpu.VMEM((nz, 8, cols), F32)
        dma = pltpu.SemaphoreType.DMA
        return pl.pallas_call(
            functools.partial(kernel, nlon, nlat, nz),
            out_shape=jax.ShapeDtypeStruct(state.shape, F32),
            in_specs=[pl.BlockSpec(memory_space=pltpu.HBM)] * 2,
            out_specs=pl.BlockSpec(memory_space=pltpu.VMEM),
            scratch_shapes=[
                pltpu.VMEM((nz, 4, rows + 16, cols), F32),
                pltpu.VMEM((nz, 4, rows + 16, cols), F32),
                pltpu.VMEM((nz, 4, rows, cols), F32),
                pltpu.VMEM((nz, 4, rows, cols), F32),
                pltpu.VMEM((rows + 16, cols), jnp.int32),
                pltpu.VMEM((5, rows, cols), jnp.int32),
                pltpu.VMEM((3, nz, 8, cols), F32),
                edge, edge, edge, edge, edge, edge, edge,
                pltpu.VMEM((nz, 4, cols), F32),
                pltpu.VMEM((nz, 4, cols), F32),
                pltpu.VMEM((1, cols), jnp.int32),
                pltpu.VMEM((2, 1, cols), jnp.int32),
                pltpu.VMEM((8, cols), jnp.int32),
                pltpu.VMEM((8, cols), jnp.int32),
                pltpu.VMEM((2, 4, rows, cols), F32),
                pltpu.VMEM((2, 4, rows, cols), F32),
                pltpu.VMEM((2, 4, rows, cols), F32),
                pltpu.VMEM((2, 4, rows, cols), F32),
                pltpu.VMEM((2, 4, rows, cols), F32),
                dma((4,)), dma((20,)), dma((20,)), dma((4,)), dma((4,)), dma((2,)), dma((2,)),
            ],
            compiler_params=pltpu.CompilerParams(
                collective_id=0, has_side_effects=True, vmem_limit_bytes=50 << 20
            ),
        )(state, depth_levels)

    return jax.shard_map(
        on_device,
        mesh=mesh,
        in_specs=(P(None, None, "lat", "lon"), P("lat", "lon")),
        out_specs=P(None, None, "lat", "lon"),
        check_vma=False,
    )
```

```python
import functools

import jax
import jax.numpy as jnp
from jax import lax
from jax.experimental import pallas as pl
from jax.experimental.pallas import tpu as pltpu
from jax.sharding import PartitionSpec as P

MESH = pl.DeviceIdType.MESH
F32 = jnp.float32
MIX = 64.0
ADV = 0.25
SPR = 0.15
PAD = 8
PARTS = 5


def kernel(nlon, nlat, nz, x, dep, out,
           st1, st2, vf, pb, dpad, dm, tab,
           xc, g1, g2, pe, ve, xe, xe2, h1, h2, hd, gd, dge, dce,
           cw, ce, hw, he, ca, cx,
           lsem, ssem, rsem, csem, crsem, dsem, bsem):
    rows = x.shape[2]
    half = rows // 8
    lon, lat = lax.axis_index("lon"), lax.axis_index("lat")
    west, east = (lax.rem(lon + nlon - 1, nlon), lat), (lax.rem(lon + 1, nlon), lat)
    north, south = (lon, lat + 1), (lon, lat - 1)
    top, near, bottom = lat == nlat - 1, lat == nlat - 2, lat == 0
    over_south, over_north = (nlon - 1 - lon, lat - 1), (nlon - 1 - lon, lat + 1)
    lane = lax.broadcasted_iota(jnp.int32, (8, 128), 1)
    sub = lax.broadcasted_iota(jnp.int32, (8, 128), 0)
    lo = sub < 4

    barrier = pltpu.get_barrier_semaphore()

    def greet(device):
        pl.semaphore_signal(barrier, inc=1, device_id=device, device_id_type=MESH)

    greet(west)
    greet(east)

    @pl.when(jnp.logical_not(top))
    def _():
        greet(north)

    @pl.when(top)
    def _():
        greet(over_south)

    @pl.when(near)
    def _():
        greet(over_north)

    @pl.when(jnp.logical_not(bottom))
    def _():
        greet(south)

    def load(i, src, dst):
        return pltpu.make_async_copy(src, dst, lsem.at[i])

    size = nz // PARTS
    parts = [(j * size, size if j < PARTS - 1 else nz - j * size) for j in range(PARTS)]
    loads = [
        load(0, dep, dpad.at[PAD:PAD + rows, :]),
        load(1, x.at[:, :, 0, :], xc.at[:, 0:4, :]),
        load(2, x.at[:, :, rows - 1, :], xc.at[:, 4:8, :]),
    ]
    body_loads = [load(3 + j, x.at[pl.ds(at, n)], st1.at[pl.ds(at, n), :, PAD:PAD + rows, :]) for j, (at, n) in enumerate(parts)]
    for one in loads[0:1] + body_loads + loads[1:3]:
        one.start()

    @pl.when(bottom)
    def _():
        pl.semaphore_wait(barrier, 3)

    @pl.when(near)
    def _():
        pl.semaphore_wait(barrier, 5)

    @pl.when(jnp.logical_not(jnp.logical_or(bottom, near)))
    def _():
        pl.semaphore_wait(barrier, 4)

    def along_lat(base, south_row, north_row, ghost, held, pieces):
        def copy(src, dst, i, device):
            return pltpu.make_async_remote_copy(src, dst, ssem.at[i], rsem.at[i], device_id=device, device_id_type=MESH)

        out = []
        for j, (at, n) in enumerate(pieces):
            part, i = pl.ds(at, n), base + 4 * j
            out.append((
                copy(north_row.at[part], ghost(0).at[part], i, north),
                copy(south_row.at[part], ghost(1).at[part], i + 1, south),
                copy(north_row.at[part], held.at[part], i + 2, over_south),
                copy(held.at[part], ghost(1).at[part], i + 3, north),
            ))
        return out

    def start_lat(lats):
        for up, down, over, on in lats:
            @pl.when(top)
            def _():
                over.start()

            @pl.when(jnp.logical_not(top))
            def _():
                up.start()

            @pl.when(jnp.logical_not(bottom))
            def _():
                down.start()

    def relay(lats, j):
        @pl.when(near)
        def _():
            lats[j][2].wait_recv()
            lats[j][3].start()

    def recv_lat(lats, j):
        up, down, over, on = lats[j]

        @pl.when(jnp.logical_not(bottom))
        def _():
            up.wait_recv()

        @pl.when(jnp.logical_not(top))
        def _():
            down.wait_recv()

        @pl.when(top)
        def _():
            on.wait_recv()

    def sent_lat(lats):
        for up, down, over, on in lats:
            @pl.when(jnp.logical_not(top))
            def _():
                up.wait_send()

            @pl.when(top)
            def _():
                over.wait_send()

            @pl.when(near)
            def _():
                on.wait_send()

            @pl.when(jnp.logical_not(bottom))
            def _():
                down.wait_send()

    def ghost_in(buf):
        return lambda e: buf.at[:, 4 * e:4 * e + 4, :]

    lat_depth = along_lat(0, dep.at[0:1, :], dep.at[rows - 1:rows, :], lambda e: gd.at[e], hd, [(0, 1)])
    lat_1 = along_lat(4, x.at[:, :, 0, :], x.at[:, :, rows - 1, :], ghost_in(g1), h1, parts)
    lat_2 = along_lat(4 + 4 * PARTS, xe.at[:, 0:4, :], xe.at[:, 4:8, :], ghost_in(g2), h2, parts)
    start_lat(lat_depth)
    start_lat(lat_1)

    zero = jnp.zeros((8, 128), F32)

    @pl.when(bottom)
    def _():
        gd[0] = jnp.zeros_like(gd[0])

        def clear(k, c):
            g1[k, 0:4] = zero[0:4]
            g2[k, 0:4] = zero[0:4]
            return c

        lax.fori_loop(0, nz, clear, 0, unroll=5)

    def clear_pads(k, c):
        for ch in range(4):
            for st in (st1, st2):
                st[k, ch, 0:PAD, :] = zero
                st[k, ch, PAD + rows:PAD + rows + 8, :] = zero
        return c

    lax.fori_loop(0, nz, clear_pads, 0, unroll=5)

    def collect(acc, i, j, value, k):
        v = pltpu.roll(value, k + 1, 1)
        acc[i] = jnp.where(lane == k + 1, v, acc[i])
        acc[j] = jnp.where(lane == k, v, acc[j])

    def collected(acc):
        n = len(acc) // 2
        return [pltpu.roll(v, 127, 1) if i < n else v for i, v in enumerate(acc)]

    def pack(st, waits):
        def body(k, acc):
            acc = list(acc)
            for ch in range(4):
                for h in range(half):
                    i = ch * half + h
                    collect(acc, i, 4 * half + i, st[k, ch, pl.ds(PAD + 8 * h, 8), :], k)
            return tuple(acc)

        acc = (zero,) * (8 * half)
        for j, (at, n) in enumerate(parts):
            waits[j].wait()
            acc = lax.fori_loop(at, at + n, body, acc, unroll=15)
        acc = collected(acc)
        for h in range(half):
            d = dpad[pl.ds(PAD + 8 * h, 8), :].astype(F32)
            acc[h] = jnp.where(lane == nz, pltpu.roll(d, nz, 1), acc[h])
            i = 4 * half + h
            acc[i] = jnp.where(lane == nz, pltpu.roll(d, nz + 1, 1), acc[i])
        return acc

    def lon_copies(step):
        def copy(src, dst, i, device):
            return pltpu.make_async_remote_copy(src, dst, csem.at[2 * step + i], crsem.at[2 * step + i], device_id=device, device_id_type=MESH)

        return [copy(cw.at[step], he.at[step], 0, west), copy(ce.at[step], hw.at[step], 1, east)]

    def send_lon(step, acc, ends):
        for ch in range(4):
            for h in range(half):
                i = ch * half + h
                cw[step, ch, pl.ds(8 * h, 8), :] = acc[i]
                ce[step, ch, pl.ds(8 * h, 8), :] = acc[4 * half + i]
        for buf, end in zip((cw, ce), ends):
            for ch in range(4):
                buf[step, ch, 0:1, :] = end[ch:ch + 1]
                buf[step, ch, rows - 1:rows, :] = end[4 + ch:5 + ch]
        copies = lon_copies(step)
        for one in copies:
            one.start()
        return copies

    loads[0].wait()
    dpad[0:PAD, :] = jnp.zeros((8, 128), jnp.int32)
    dpad[PAD + rows:PAD + rows + 8, :] = jnp.zeros((8, 128), jnp.int32)
    lon_1 = send_lon(0, pack(st1, body_loads), [])

    first, final = lane == 0, lane == 127

    def depth_maps():
        for h in range(half):
            at = pl.ds(8 * h, 8)
            d = dpad[pl.ds(PAD + 8 * h, 8), :]
            dm[0, at, :] = d
            dm[1, at, :] = jnp.where(final, 0, pltpu.roll(d, 127, 1))
            dm[2, at, :] = jnp.where(first, 0, pltpu.roll(d, 1, 1))
            dm[3, at, :] = dpad[pl.ds(PAD + 8 * h + 1, 8), :]
            dm[4, at, :] = dpad[pl.ds(PAD + 8 * h - 1, 8), :]

    total = F32(rows * nlat)

    def rotation(h):
        row = (sub + (8 * h + lat * rows)).astype(F32)
        return 0.1 + 0.4 * (row + 0.5) / total

    def dense(warm, salt, wet):
        return jnp.where(wet, 0.075 * salt - 0.025 * warm, 0.0)

    def stencil(st, make_table, lats):
        turns = [rotation(h) for h in range(half)]

        def body(k, carry):
            grad_e = list(carry[0:half])
            grad_n = list(carry[half:2 * half])
            upper = carry[2 * half]
            if make_table:
                pivot = jnp.where(k == 0, 1.0 + MIX, 1.0 + 2.0 * MIX - MIX * upper)
                inv = 1.0 / pivot
                upper = MIX * inv
                tab[0, k] = inv
                tab[1, k] = 1.0 / (pivot - MIX)
                tab[2, k] = upper
            for h in range(half):
                at = pl.ds(8 * h, 8)
                wet = [None] + [k < dm[i, at, :] for i in range(1, 5)]
                w15 = [jnp.where(m, F32(SPR), F32(0.0)) for m in wet[1:]]
                q = [st[k, ch, pl.ds(PAD + 8 * h, 8), :] for ch in range(4)]
                qe = [pltpu.roll(v, 127, 1) for v in q]
                qw = [pltpu.roll(v, 1, 1) for v in q]
                qn = [st[k, ch, pl.ds(PAD + 8 * h + 1, 8), :] for ch in range(4)]
                qs = [st[k, ch, pl.ds(PAD + 8 * h - 1, 8), :] for ch in range(4)]
                a_e = jnp.where(final, 0.0, w15[0] - ADV * qe[2])
                a_w = jnp.where(first, 0.0, w15[1] + ADV * qw[2])
                a_n = w15[2] - ADV * qn[3]
                a_s = w15[3] + ADV * qs[3]
                centre = 1.0 - (w15[0] + w15[1]) - (w15[2] + w15[3])
                grad_e[h] = grad_e[h] + (dense(qe[0], qe[1], wet[1]) - dense(qw[0], qw[1], wet[2]))
                grad_n[h] = grad_n[h] + (dense(qn[0], qn[1], wet[3]) - dense(qs[0], qs[1], wet[4]))
                turn = turns[h]
                for ch in range(4):
                    p = (centre * q[ch] + a_e * qe[ch]) + (a_w * qw[ch] + a_n * qn[ch]) + a_s * qs[ch]
                    if ch == 2:
                        p = p + (turn * q[3] - grad_e[h])
                    if ch == 3:
                        p = p - (turn * q[2] + grad_n[h])
                    pb[k, ch, at, :] = p
            return tuple(grad_e + grad_n + [upper])

        carry = (zero,) * (2 * half + 1)
        for j, (at, n) in enumerate(parts):
            carry = lax.fori_loop(at, at + n, body, carry, unroll=5)
            relay(lats, j)
        copies = [pltpu.make_async_copy(pb.at[:, :, 0, :], pe.at[:, 0:4, :], dsem.at[0]),
                  pltpu.make_async_copy(pb.at[:, :, rows - 1, :], pe.at[:, 4:8, :], dsem.at[1])]
        for one in copies:
            one.start()
        return copies

    def columns(step):
        for h in range(half):
            at = pl.ds(8 * h, 8)
            adds = []
            for halo, own, way in ((hw, cw, 1.0), (he, ce, -1.0)):
                deep = jnp.broadcast_to(halo[0, 0, at, nz:nz + 1], (8, 128)).astype(jnp.int32)
                wet = lane < deep
                w15 = jnp.where(wet, F32(SPR), F32(0.0))
                q = [halo[step, ch, at, :] for ch in range(4)]
                coef = w15 + (way * ADV) * q[2]
                push = dense(q[0], q[1], wet)
                shift = 1
                while shift < nz:
                    push = push + jnp.where(lane >= shift, pltpu.roll(push, shift, 1), 0.0)
                    shift *= 2
                add = [coef * q[ch] - w15 * own[step, ch, at, :] for ch in range(4)]
                add[2] = add[2] + way * push
                adds.append(add)
            even = lax.rem(lane, 2) == 0
            for ch in range(4):
                w, e = adds[0][ch], pltpu.roll(adds[1][ch], 127, 1)
                ca[0, ch, at, :] = jnp.where(even, w, e)
                ca[1, ch, at, :] = jnp.where(even, e, w)
        for odd in range(2):
            for ch in range(4):
                cx[odd, ch:ch + 1, :] = ca[odd, ch, 0:1, :]
                cx[odd, 4 + ch:5 + ch, :] = ca[odd, ch, rows - 1:rows, :]

    outer = jnp.logical_or(first, final)

    def inverse(k, depth):
        inv = jnp.where((k + 1) == depth, tab[1, k], tab[0, k])
        return jnp.where(k < depth, inv, 0.0)

    def sweeps(dst, dst_row, gather):
        def forward(k, carry):
            new = list(carry)
            back = lax.rem(128 - k, 128)
            odd = lax.rem(k, 2)
            for h in range(half):
                at = pl.ds(8 * h, 8)
                inv = inverse(k, dm[0, at, :])
                low = MIX * inv
                for ch in range(4):
                    p = pb[k, ch, at, :] + jnp.where(outer, pltpu.roll(ca[odd, ch, at, :], back, 1), 0.0)
                    i = ch * half + h
                    new[i] = p * inv - low * new[i]
                    vf[k, ch, at, :] = new[i]
            return tuple(new)

        lax.fori_loop(0, nz, forward, (zero,) * (4 * half), unroll=15)

        def backward(j, carry):
            k = nz - 1 - j
            up = tab[2, k]
            new = list(carry)
            for ch in range(4):
                for h in range(half):
                    i = ch * half + h
                    s = vf[k, ch, pl.ds(8 * h, 8), :] - up * carry[i]
                    dst[k, ch, pl.ds(dst_row + 8 * h, 8), :] = s
                    new[i] = s
                    if gather:
                        collect(new, 4 * half + i, 8 * half + i, s, k)
            return tuple(new)

        count = (12 if gather else 4) * half
        carry = lax.fori_loop(0, nz, backward, (zero,) * count, unroll=15)
        return collected(carry[4 * half:])

    flip = jnp.logical_and(top, sub >= 4)
    index = jnp.where(flip, 127 - lane, lane)
    sign = jnp.where(jnp.logical_and(flip, lax.rem(sub, 4) >= 2), F32(-1.0), F32(1.0))
    slope = jnp.where(lo, F32(ADV), jnp.where(top, F32(ADV), F32(-ADV)))
    push = jnp.where(sub == 3, F32(1.0), jnp.where(sub == 7, F32(-1.0), F32(0.0)))

    def mirrored(v):
        return jnp.take_along_axis(v, index, axis=1)

    def edges(ghost, centre, solved, lats, gather):
        def both(k, c):
            return mirrored(jnp.where(lo, ghost[k, c:c + 1, :], ghost[k, c + 4:c + 5, :]))

        def forward(k, carry):
            prev, grad = carry
            g = mirrored(ghost[k])
            warm, salt, vel = both(k, 0), both(k, 1), both(k, 3)
            wet = k < dge[...]
            w15 = jnp.where(wet, F32(SPR), 0.0)
            grad = grad + push * dense(warm, salt, wet)
            side = jnp.where(outer, pltpu.roll(cx[lax.rem(k, 2)], lax.rem(128 - k, 128), 1), 0.0)
            p = (pe[k] + side) + ((w15 + slope * vel) * (sign * g) - w15 * centre[k]) + grad
            inv = inverse(k, dce[...])
            prev = p * inv - (MIX * inv) * prev
            ve[k] = prev
            return prev, grad

        carry = (zero, zero)
        for j, (at, n) in enumerate(parts):
            recv_lat(lats, j)
            carry = lax.fori_loop(at, at + n, forward, carry, unroll=15)

        def backward(j, carry):
            k = nz - 1 - j
            new = list(carry)
            new[0] = ve[k] - tab[2, k] * carry[0]
            solved[k] = new[0]
            if gather:
                collect(new, 1, 2, new[0], k)
            return tuple(new)

        carry = lax.fori_loop(0, nz, backward, (zero,) * (3 if gather else 1), unroll=25)
        return collected(carry[1:])

    depth_maps()
    relay(lat_depth, 0)
    copies = stencil(st1, True, lat_1)
    for one in lon_1:
        one.wait_recv()
    columns(0)
    for one in copies + loads[1:3]:
        one.wait()
    recv_lat(lat_depth, 0)
    dce[...] = jnp.where(lo, dm[0, 0:1, :], dm[0, rows - 1:rows, :])
    dge[...] = mirrored(jnp.where(lo, gd[0], gd[1]).astype(F32)).astype(jnp.int32)
    ends = edges(g1, xc, xe, lat_1, True)
    start_lat(lat_2)
    lon_2 = send_lon(1, sweeps(st2, PAD, True), ends)
    patch = [pltpu.make_async_copy(xe.at[:, 0:4, :], st2.at[:, :, PAD, :], bsem.at[0]),
             pltpu.make_async_copy(xe.at[:, 4:8, :], st2.at[:, :, PAD + rows - 1, :], bsem.at[1])]
    for one in patch:
        one.start()
    for one in patch:
        one.wait()
    copies = stencil(st2, False, lat_2)
    for one in lon_2:
        one.wait_recv()
    columns(1)
    sweeps(out, 0, False)
    for one in copies:
        one.wait()
    edges(g2, xe, xe2, lat_2, False)
    last = [pltpu.make_async_copy(xe2.at[:, 0:4, :], out.at[:, :, 0, :], bsem.at[0]),
            pltpu.make_async_copy(xe2.at[:, 4:8, :], out.at[:, :, rows - 1, :], bsem.at[1])]
    for one in last:
        one.start()
    for one in lon_1 + lon_2:
        one.wait_send()
    sent_lat(lat_depth)
    sent_lat(lat_1)
    sent_lat(lat_2)
    for one in last:
        one.wait()


def solution(mesh):
    nlon, nlat = mesh.shape["lon"], mesh.shape["lat"]

    def on_device(state, depth_levels):
        nz, _, rows, cols = state.shape
        edge = pltpu.VMEM((nz, 8, cols), F32)
        dma = pltpu.SemaphoreType.DMA
        return pl.pallas_call(
            functools.partial(kernel, nlon, nlat, nz),
            out_shape=jax.ShapeDtypeStruct(state.shape, F32),
            in_specs=[pl.BlockSpec(memory_space=pltpu.HBM)] * 2,
            out_specs=pl.BlockSpec(memory_space=pltpu.VMEM),
            scratch_shapes=[
                pltpu.VMEM((nz, 4, rows + 16, cols), F32),
                pltpu.VMEM((nz, 4, rows + 16, cols), F32),
                pltpu.VMEM((nz, 4, rows, cols), F32),
                pltpu.VMEM((nz, 4, rows, cols), F32),
                pltpu.VMEM((rows + 16, cols), jnp.int32),
                pltpu.VMEM((5, rows, cols), jnp.int32),
                pltpu.VMEM((3, nz, 8, cols), F32),
                edge, edge, edge, edge, edge, edge, edge,
                pltpu.VMEM((nz, 4, cols), F32),
                pltpu.VMEM((nz, 4, cols), F32),
                pltpu.VMEM((1, cols), jnp.int32),
                pltpu.VMEM((2, 1, cols), jnp.int32),
                pltpu.VMEM((8, cols), jnp.int32),
                pltpu.VMEM((8, cols), jnp.int32),
                pltpu.VMEM((2, 4, rows, cols), F32),
                pltpu.VMEM((2, 4, rows, cols), F32),
                pltpu.VMEM((2, 4, rows, cols), F32),
                pltpu.VMEM((2, 4, rows, cols), F32),
                pltpu.VMEM((2, 4, rows, cols), F32),
                pltpu.VMEM((2, 8, cols), F32),
                dma((3 + PARTS,)), dma((4 + 8 * PARTS,)), dma((4 + 8 * PARTS,)), dma((4,)), dma((4,)), dma((2,)), dma((2,)),
            ],
            compiler_params=pltpu.CompilerParams(
                collective_id=0, has_side_effects=True, vmem_limit_bytes=50 << 20
            ),
        )(state, depth_levels)

    return jax.shard_map(
        on_device,
        mesh=mesh,
        in_specs=(P(None, None, "lat", "lon"), P("lat", "lon")),
        out_specs=P(None, None, "lat", "lon"),
        check_vma=False,
    )
```

```python
import functools

import jax
import jax.numpy as jnp
from jax import lax
from jax.experimental import pallas as pl
from jax.experimental.pallas import tpu as pltpu
from jax.sharding import PartitionSpec as P

MESH = pl.DeviceIdType.MESH
F32 = jnp.float32
MIX = 64.0
ADV = 0.25
SPR = 0.15
PAD = 8
PARTS = 5


def kernel(nlon, nlat, nz, x, dep, out,
           st1, st2, vf, pb, dpad, dm, tab,
           xc, g1, g2, pe, ve, xe, xe2, h1, h2, hd, gd, dge, dce,
           cw, ce, hw, he, ca, cx,
           lsem, ssem, rsem, csem, crsem, dsem, bsem):
    rows = x.shape[2]
    half = rows // 8
    lon, lat = lax.axis_index("lon"), lax.axis_index("lat")
    west, east = (lax.rem(lon + nlon - 1, nlon), lat), (lax.rem(lon + 1, nlon), lat)
    north, south = (lon, lat + 1), (lon, lat - 1)
    top, near, bottom = lat == nlat - 1, lat == nlat - 2, lat == 0
    over_south, over_north = (nlon - 1 - lon, lat - 1), (nlon - 1 - lon, lat + 1)
    lane = lax.broadcasted_iota(jnp.int32, (8, 128), 1)
    sub = lax.broadcasted_iota(jnp.int32, (8, 128), 0)
    lo = sub < 4

    barrier = pltpu.get_barrier_semaphore()

    def greet(device):
        pl.semaphore_signal(barrier, inc=1, device_id=device, device_id_type=MESH)

    greet(west)
    greet(east)

    @pl.when(jnp.logical_not(top))
    def _():
        greet(north)

    @pl.when(top)
    def _():
        greet(over_south)

    @pl.when(near)
    def _():
        greet(over_north)

    @pl.when(jnp.logical_not(bottom))
    def _():
        greet(south)

    def load(i, src, dst):
        return pltpu.make_async_copy(src, dst, lsem.at[i])

    size = nz // PARTS
    parts = [(j * size, size if j < PARTS - 1 else nz - j * size) for j in range(PARTS)]
    loads = [
        load(0, dep, dpad.at[PAD:PAD + rows, :]),
        load(1, x.at[:, :, 0, :], xc.at[:, 0:4, :]),
        load(2, x.at[:, :, rows - 1, :], xc.at[:, 4:8, :]),
    ]
    body_loads = [load(3 + j, x.at[pl.ds(at, n)], st1.at[pl.ds(at, n), :, PAD:PAD + rows, :]) for j, (at, n) in enumerate(parts)]
    for one in loads[0:1] + body_loads + loads[1:3]:
        one.start()

    @pl.when(bottom)
    def _():
        pl.semaphore_wait(barrier, 3)

    @pl.when(near)
    def _():
        pl.semaphore_wait(barrier, 5)

    @pl.when(jnp.logical_not(jnp.logical_or(bottom, near)))
    def _():
        pl.semaphore_wait(barrier, 4)

    def along_lat(base, south_row, north_row, ghost, held, pieces):
        def copy(src, dst, i, device):
            return pltpu.make_async_remote_copy(src, dst, ssem.at[i], rsem.at[i], device_id=device, device_id_type=MESH)

        out = []
        for j, (at, n) in enumerate(pieces):
            part, i = pl.ds(at, n), base + 4 * j
            out.append((
                copy(north_row.at[part], ghost(0).at[part], i, north),
                copy(south_row.at[part], ghost(1).at[part], i + 1, south),
                copy(north_row.at[part], held.at[part], i + 2, over_south),
                copy(held.at[part], ghost(1).at[part], i + 3, north),
            ))
        return out

    def start_lat(lats):
        for up, down, over, on in lats:
            @pl.when(top)
            def _():
                over.start()

            @pl.when(jnp.logical_not(top))
            def _():
                up.start()

            @pl.when(jnp.logical_not(bottom))
            def _():
                down.start()

    def relay(lats, j):
        @pl.when(near)
        def _():
            lats[j][2].wait_recv()
            lats[j][3].start()

    def recv_lat(lats, j):
        up, down, over, on = lats[j]

        @pl.when(jnp.logical_not(bottom))
        def _():
            up.wait_recv()

        @pl.when(jnp.logical_not(top))
        def _():
            down.wait_recv()

        @pl.when(top)
        def _():
            on.wait_recv()

    def sent_lat(lats):
        for up, down, over, on in lats:
            @pl.when(jnp.logical_not(top))
            def _():
                up.wait_send()

            @pl.when(top)
            def _():
                over.wait_send()

            @pl.when(near)
            def _():
                on.wait_send()

            @pl.when(jnp.logical_not(bottom))
            def _():
                down.wait_send()

    def ghost_in(buf):
        return lambda e: buf.at[:, 4 * e:4 * e + 4, :]

    lat_depth = along_lat(0, dep.at[0:1, :], dep.at[rows - 1:rows, :], lambda e: gd.at[e], hd, [(0, 1)])
    lat_1 = along_lat(4, x.at[:, :, 0, :], x.at[:, :, rows - 1, :], ghost_in(g1), h1, parts)
    lat_2 = along_lat(4 + 4 * PARTS, xe.at[:, 0:4, :], xe.at[:, 4:8, :], ghost_in(g2), h2, parts)
    start_lat(lat_depth)
    start_lat(lat_1)

    zero = jnp.zeros((8, 128), F32)

    def collect(acc, i, j, value, k):
        v = pltpu.roll(value, k + 1, 1)
        acc[i] = jnp.where(lane == k + 1, v, acc[i])
        acc[j] = jnp.where(lane == k, v, acc[j])

    def collected(acc):
        n = len(acc) // 2
        return [pltpu.roll(v, 127, 1) if i < n else v for i, v in enumerate(acc)]

    def pack(st, waits):
        def body(k, acc):
            acc = list(acc)
            for ch in range(4):
                for h in range(half):
                    i = ch * half + h
                    collect(acc, i, 4 * half + i, st[k, ch, pl.ds(PAD + 8 * h, 8), :], k)
            return tuple(acc)

        acc = (zero,) * (8 * half)
        for j, (at, n) in enumerate(parts):
            waits[j].wait()
            acc = lax.fori_loop(at, at + n, body, acc, unroll=15)
        acc = collected(acc)
        for h in range(half):
            d = dpad[pl.ds(PAD + 8 * h, 8), :].astype(F32)
            acc[h] = jnp.where(lane == nz, pltpu.roll(d, nz, 1), acc[h])
            i = 4 * half + h
            acc[i] = jnp.where(lane == nz, pltpu.roll(d, nz + 1, 1), acc[i])
        return acc

    def lon_copies(step):
        def copy(src, dst, i, device):
            return pltpu.make_async_remote_copy(src, dst, csem.at[2 * step + i], crsem.at[2 * step + i], device_id=device, device_id_type=MESH)

        return [copy(cw.at[step], he.at[step], 0, west), copy(ce.at[step], hw.at[step], 1, east)]

    def send_lon(step, acc, ends):
        for ch in range(4):
            for h in range(half):
                i = ch * half + h
                cw[step, ch, pl.ds(8 * h, 8), :] = acc[i]
                ce[step, ch, pl.ds(8 * h, 8), :] = acc[4 * half + i]
        for buf, end in zip((cw, ce), ends):
            for ch in range(4):
                buf[step, ch, 0:1, :] = end[ch:ch + 1]
                buf[step, ch, rows - 1:rows, :] = end[4 + ch:5 + ch]
        copies = lon_copies(step)
        for one in copies:
            one.start()
        return copies

    loads[0].wait()
    dpad[0:PAD, :] = jnp.zeros((8, 128), jnp.int32)
    dpad[PAD + rows:PAD + rows + 8, :] = jnp.zeros((8, 128), jnp.int32)
    lon_1 = send_lon(0, pack(st1, body_loads), [])

    @pl.when(bottom)
    def _():
        gd[0] = jnp.zeros_like(gd[0])

        def clear(k, c):
            g1[k, 0:4] = zero[0:4]
            g2[k, 0:4] = zero[0:4]
            return c

        lax.fori_loop(0, nz, clear, 0, unroll=5)

    def clear_pads(k, c):
        for ch in range(4):
            for st in (st1, st2):
                st[k, ch, 0:PAD, :] = zero
                st[k, ch, PAD + rows:PAD + rows + 8, :] = zero
        return c

    lax.fori_loop(0, nz, clear_pads, 0, unroll=5)

    first, final = lane == 0, lane == 127

    def depth_maps():
        for h in range(half):
            at = pl.ds(8 * h, 8)
            d = dpad[pl.ds(PAD + 8 * h, 8), :]
            dm[0, at, :] = d
            dm[1, at, :] = jnp.where(final, 0, pltpu.roll(d, 127, 1))
            dm[2, at, :] = jnp.where(first, 0, pltpu.roll(d, 1, 1))
            dm[3, at, :] = dpad[pl.ds(PAD + 8 * h + 1, 8), :]
            dm[4, at, :] = dpad[pl.ds(PAD + 8 * h - 1, 8), :]

    total = F32(rows * nlat)

    def rotation(h):
        row = (sub + (8 * h + lat * rows)).astype(F32)
        return 0.1 + 0.4 * (row + 0.5) / total

    def dense(warm, salt, wet):
        return jnp.where(wet, 0.075 * salt - 0.025 * warm, 0.0)

    def stencil(st, make_table, lats):
        turns = [rotation(h) for h in range(half)]

        def body(k, carry):
            grad_e = list(carry[0:half])
            grad_n = list(carry[half:2 * half])
            upper = carry[2 * half]
            if make_table:
                pivot = jnp.where(k == 0, 1.0 + MIX, 1.0 + 2.0 * MIX - MIX * upper)
                inv = 1.0 / pivot
                upper = MIX * inv
                tab[0, k] = inv
                tab[1, k] = 1.0 / (pivot - MIX)
                tab[2, k] = upper
            for h in range(half):
                at = pl.ds(8 * h, 8)
                wet = [None] + [k < dm[i, at, :] for i in range(1, 5)]
                w15 = [jnp.where(m, F32(SPR), F32(0.0)) for m in wet[1:]]
                q = [st[k, ch, pl.ds(PAD + 8 * h, 8), :] for ch in range(4)]
                qe = [pltpu.roll(v, 127, 1) for v in q]
                qw = [pltpu.roll(v, 1, 1) for v in q]
                qn = [st[k, ch, pl.ds(PAD + 8 * h + 1, 8), :] for ch in range(4)]
                qs = [st[k, ch, pl.ds(PAD + 8 * h - 1, 8), :] for ch in range(4)]
                a_e = jnp.where(final, 0.0, w15[0] - ADV * qe[2])
                a_w = jnp.where(first, 0.0, w15[1] + ADV * qw[2])
                a_n = w15[2] - ADV * qn[3]
                a_s = w15[3] + ADV * qs[3]
                centre = 1.0 - (w15[0] + w15[1]) - (w15[2] + w15[3])
                grad_e[h] = grad_e[h] + (dense(qe[0], qe[1], wet[1]) - dense(qw[0], qw[1], wet[2]))
                grad_n[h] = grad_n[h] + (dense(qn[0], qn[1], wet[3]) - dense(qs[0], qs[1], wet[4]))
                turn = turns[h]
                for ch in range(4):
                    p = (centre * q[ch] + a_e * qe[ch]) + (a_w * qw[ch] + a_n * qn[ch]) + a_s * qs[ch]
                    if ch == 2:
                        p = p + (turn * q[3] - grad_e[h])
                    if ch == 3:
                        p = p - (turn * q[2] + grad_n[h])
                    pb[k, ch, at, :] = p
            return tuple(grad_e + grad_n + [upper])

        carry = (zero,) * (2 * half + 1)
        for j, (at, n) in enumerate(parts):
            carry = lax.fori_loop(at, at + n, body, carry, unroll=5)
            relay(lats, j)
        copies = [pltpu.make_async_copy(pb.at[:, :, 0, :], pe.at[:, 0:4, :], dsem.at[0]),
                  pltpu.make_async_copy(pb.at[:, :, rows - 1, :], pe.at[:, 4:8, :], dsem.at[1])]
        for one in copies:
            one.start()
        return copies

    def columns(step):
        for h in range(half):
            at = pl.ds(8 * h, 8)
            adds = []
            for halo, own, way in ((hw, cw, 1.0), (he, ce, -1.0)):
                deep = jnp.broadcast_to(halo[0, 0, at, nz:nz + 1], (8, 128)).astype(jnp.int32)
                wet = lane < deep
                w15 = jnp.where(wet, F32(SPR), F32(0.0))
                q = [halo[step, ch, at, :] for ch in range(4)]
                coef = w15 + (way * ADV) * q[2]
                push = dense(q[0], q[1], wet)
                shift = 1
                while shift < nz:
                    push = push + jnp.where(lane >= shift, pltpu.roll(push, shift, 1), 0.0)
                    shift *= 2
                add = [coef * q[ch] - w15 * own[step, ch, at, :] for ch in range(4)]
                add[2] = add[2] + way * push
                adds.append(add)
            even = lax.rem(lane, 2) == 0
            for ch in range(4):
                w, e = adds[0][ch], pltpu.roll(adds[1][ch], 127, 1)
                ca[0, ch, at, :] = jnp.where(even, w, e)
                ca[1, ch, at, :] = jnp.where(even, e, w)
        for odd in range(2):
            for ch in range(4):
                cx[odd, ch:ch + 1, :] = ca[odd, ch, 0:1, :]
                cx[odd, 4 + ch:5 + ch, :] = ca[odd, ch, rows - 1:rows, :]

    outer = jnp.logical_or(first, final)

    def inverse(k, depth):
        inv = jnp.where((k + 1) == depth, tab[1, k], tab[0, k])
        return jnp.where(k < depth, inv, 0.0)

    def sweeps(dst, dst_row, gather):
        def forward(k, carry):
            new = list(carry)
            back = lax.rem(128 - k, 128)
            odd = lax.rem(k, 2)
            for h in range(half):
                at = pl.ds(8 * h, 8)
                inv = inverse(k, dm[0, at, :])
                low = MIX * inv
                for ch in range(4):
                    p = pb[k, ch, at, :] + jnp.where(outer, pltpu.roll(ca[odd, ch, at, :], back, 1), 0.0)
                    i = ch * half + h
                    new[i] = p * inv - low * new[i]
                    vf[k, ch, at, :] = new[i]
            return tuple(new)

        lax.fori_loop(0, nz, forward, (zero,) * (4 * half), unroll=15)

        def backward(j, carry):
            k = nz - 1 - j
            up = tab[2, k]
            new = list(carry)
            for ch in range(4):
                for h in range(half):
                    i = ch * half + h
                    s = vf[k, ch, pl.ds(8 * h, 8), :] - up * carry[i]
                    dst[k, ch, pl.ds(dst_row + 8 * h, 8), :] = s
                    new[i] = s
                    if gather:
                        collect(new, 4 * half + i, 8 * half + i, s, k)
            return tuple(new)

        count = (12 if gather else 4) * half
        carry = lax.fori_loop(0, nz, backward, (zero,) * count, unroll=15)
        return collected(carry[4 * half:])

    flip = jnp.logical_and(top, sub >= 4)
    index = jnp.where(flip, 127 - lane, lane)
    sign = jnp.where(jnp.logical_and(flip, lax.rem(sub, 4) >= 2), F32(-1.0), F32(1.0))
    slope = jnp.where(lo, F32(ADV), jnp.where(top, F32(ADV), F32(-ADV)))
    push = jnp.where(sub == 3, F32(1.0), jnp.where(sub == 7, F32(-1.0), F32(0.0)))

    def mirrored(v):
        return jnp.take_along_axis(v, index, axis=1)

    def edges(ghost, centre, solved, lats, gather, into=None):
        def both(k, c):
            return mirrored(jnp.where(lo, ghost[k, c:c + 1, :], ghost[k, c + 4:c + 5, :]))

        def forward(k, carry):
            prev, grad = carry
            g = mirrored(ghost[k])
            warm, salt, vel = both(k, 0), both(k, 1), both(k, 3)
            wet = k < dge[...]
            w15 = jnp.where(wet, F32(SPR), 0.0)
            grad = grad + push * dense(warm, salt, wet)
            side = jnp.where(outer, pltpu.roll(cx[lax.rem(k, 2)], lax.rem(128 - k, 128), 1), 0.0)
            p = (pe[k] + side) + ((w15 + slope * vel) * (sign * g) - w15 * centre[k]) + grad
            inv = inverse(k, dce[...])
            prev = p * inv - (MIX * inv) * prev
            ve[k] = prev
            return prev, grad

        carry = (zero, zero)
        for j, (at, n) in enumerate(parts):
            recv_lat(lats, j)
            carry = lax.fori_loop(at, at + n, forward, carry, unroll=15)

        def backward(j, carry):
            k = nz - 1 - j
            new = list(carry)
            new[0] = ve[k] - tab[2, k] * carry[0]
            solved[k] = new[0]
            if into is not None:
                for ch in range(4):
                    into[k, ch, 0:1, :] = new[0][ch:ch + 1]
                    into[k, ch, rows - 1:rows, :] = new[0][4 + ch:5 + ch]
            if gather:
                collect(new, 1, 2, new[0], k)
            return tuple(new)

        carry = lax.fori_loop(0, nz, backward, (zero,) * (3 if gather else 1), unroll=25)
        return collected(carry[1:])

    depth_maps()
    relay(lat_depth, 0)
    copies = stencil(st1, True, lat_1)
    for one in lon_1:
        one.wait_recv()
    columns(0)
    for one in copies + loads[1:3]:
        one.wait()
    recv_lat(lat_depth, 0)
    dce[...] = jnp.where(lo, dm[0, 0:1, :], dm[0, rows - 1:rows, :])
    dge[...] = mirrored(jnp.where(lo, gd[0], gd[1]).astype(F32)).astype(jnp.int32)
    ends = edges(g1, xc, xe, lat_1, True)
    start_lat(lat_2)
    lon_2 = send_lon(1, sweeps(st2, PAD, True), ends)
    patch = [pltpu.make_async_copy(xe.at[:, 0:4, :], st2.at[:, :, PAD, :], bsem.at[0]),
             pltpu.make_async_copy(xe.at[:, 4:8, :], st2.at[:, :, PAD + rows - 1, :], bsem.at[1])]
    for one in patch:
        one.start()
    for one in patch:
        one.wait()
    copies = stencil(st2, False, lat_2)
    for one in lon_2:
        one.wait_recv()
    columns(1)
    sweeps(out, 0, False)
    for one in copies:
        one.wait()
    edges(g2, xe, xe2, lat_2, False, out)
    for one in lon_1 + lon_2:
        one.wait_send()
    sent_lat(lat_depth)
    sent_lat(lat_1)
    sent_lat(lat_2)


def solution(mesh):
    nlon, nlat = mesh.shape["lon"], mesh.shape["lat"]

    def on_device(state, depth_levels):
        nz, _, rows, cols = state.shape
        edge = pltpu.VMEM((nz, 8, cols), F32)
        dma = pltpu.SemaphoreType.DMA
        return pl.pallas_call(
            functools.partial(kernel, nlon, nlat, nz),
            out_shape=jax.ShapeDtypeStruct(state.shape, F32),
            in_specs=[pl.BlockSpec(memory_space=pltpu.HBM)] * 2,
            out_specs=pl.BlockSpec(memory_space=pltpu.VMEM),
            scratch_shapes=[
                pltpu.VMEM((nz, 4, rows + 16, cols), F32),
                pltpu.VMEM((nz, 4, rows + 16, cols), F32),
                pltpu.VMEM((nz, 4, rows, cols), F32),
                pltpu.VMEM((nz, 4, rows, cols), F32),
                pltpu.VMEM((rows + 16, cols), jnp.int32),
                pltpu.VMEM((5, rows, cols), jnp.int32),
                pltpu.VMEM((3, nz, 8, cols), F32),
                edge, edge, edge, edge, edge, edge, edge,
                pltpu.VMEM((nz, 4, cols), F32),
                pltpu.VMEM((nz, 4, cols), F32),
                pltpu.VMEM((1, cols), jnp.int32),
                pltpu.VMEM((2, 1, cols), jnp.int32),
                pltpu.VMEM((8, cols), jnp.int32),
                pltpu.VMEM((8, cols), jnp.int32),
                pltpu.VMEM((2, 4, rows, cols), F32),
                pltpu.VMEM((2, 4, rows, cols), F32),
                pltpu.VMEM((2, 4, rows, cols), F32),
                pltpu.VMEM((2, 4, rows, cols), F32),
                pltpu.VMEM((2, 4, rows, cols), F32),
                pltpu.VMEM((2, 8, cols), F32),
                dma((3 + PARTS,)), dma((4 + 8 * PARTS,)), dma((4 + 8 * PARTS,)), dma((4,)), dma((4,)), dma((2,)), dma((2,)),
            ],
            compiler_params=pltpu.CompilerParams(
                collective_id=0, has_side_effects=True, vmem_limit_bytes=50 << 20
            ),
        )(state, pltpu.with_memory_space_constraint(depth_levels, pltpu.HBM))

    return jax.shard_map(
        on_device,
        mesh=mesh,
        in_specs=(P(None, None, "lat", "lon"), P("lat", "lon")),
        out_specs=P(None, None, "lat", "lon"),
        check_vma=False,
    )
```

```python
import functools

import jax
import jax.numpy as jnp
from jax import lax
from jax.experimental import pallas as pl
from jax.experimental.pallas import tpu as pltpu
from jax.sharding import PartitionSpec as P

MESH = pl.DeviceIdType.MESH
F32 = jnp.float32
MIX = 64.0
ADV = 0.25
SPR = 0.15
PAD = 8
PARTS = 5


def kernel(nlon, nlat, nz, x, dep, out,
           st1, st2, vf, pb, dpad, dm, tab,
           xc, g1, g2, pe, ve, xe, xe2, h1, h2, hd, gd, dge, dce,
           cw, ce, hw, he, ca, cx, cp,
           lsem, ssem, rsem, csem, crsem, dsem, bsem):
    rows = x.shape[2]
    half = rows // 8
    lon, lat = lax.axis_index("lon"), lax.axis_index("lat")
    west, east = (lax.rem(lon + nlon - 1, nlon), lat), (lax.rem(lon + 1, nlon), lat)
    north, south = (lon, lat + 1), (lon, lat - 1)
    top, near, bottom = lat == nlat - 1, lat == nlat - 2, lat == 0
    over_south, over_north = (nlon - 1 - lon, lat - 1), (nlon - 1 - lon, lat + 1)
    lane = lax.broadcasted_iota(jnp.int32, (8, 128), 1)
    sub = lax.broadcasted_iota(jnp.int32, (8, 128), 0)
    lo = sub < 4

    barrier = pltpu.get_barrier_semaphore()

    def greet(device):
        pl.semaphore_signal(barrier, inc=1, device_id=device, device_id_type=MESH)

    greet(west)
    greet(east)

    @pl.when(jnp.logical_not(top))
    def _():
        greet(north)

    @pl.when(top)
    def _():
        greet(over_south)

    @pl.when(near)
    def _():
        greet(over_north)

    @pl.when(jnp.logical_not(bottom))
    def _():
        greet(south)

    def load(i, src, dst):
        return pltpu.make_async_copy(src, dst, lsem.at[i])

    size = nz // PARTS
    parts = [(j * size, size if j < PARTS - 1 else nz - j * size) for j in range(PARTS)]
    loads = [
        load(0, dep, dpad.at[PAD:PAD + rows, :]),
        load(1, x.at[:, :, 0, :], xc.at[:, 0:4, :]),
        load(2, x.at[:, :, rows - 1, :], xc.at[:, 4:8, :]),
    ]
    body_loads = [load(3 + j, x.at[pl.ds(at, n)], st1.at[pl.ds(at, n), :, PAD:PAD + rows, :]) for j, (at, n) in enumerate(parts)]
    for one in loads[0:1] + body_loads + loads[1:3]:
        one.start()

    @pl.when(bottom)
    def _():
        pl.semaphore_wait(barrier, 3)

    @pl.when(near)
    def _():
        pl.semaphore_wait(barrier, 5)

    @pl.when(jnp.logical_not(jnp.logical_or(bottom, near)))
    def _():
        pl.semaphore_wait(barrier, 4)

    def along_lat(base, south_row, north_row, ghost, held, pieces):
        def copy(src, dst, i, device):
            return pltpu.make_async_remote_copy(src, dst, ssem.at[i], rsem.at[i], device_id=device, device_id_type=MESH)

        out = []
        for j, (at, n) in enumerate(pieces):
            part, i = pl.ds(at, n), base + 4 * j
            out.append((
                copy(north_row.at[part], ghost(0).at[part], i, north),
                copy(south_row.at[part], ghost(1).at[part], i + 1, south),
                copy(north_row.at[part], held.at[part], i + 2, over_south),
                copy(held.at[part], ghost(1).at[part], i + 3, north),
            ))
        return out

    def start_lat(lats):
        for up, down, over, on in lats:
            @pl.when(top)
            def _():
                over.start()

            @pl.when(jnp.logical_not(top))
            def _():
                up.start()

            @pl.when(jnp.logical_not(bottom))
            def _():
                down.start()

    def relay(lats, j):
        @pl.when(near)
        def _():
            lats[j][2].wait_recv()
            lats[j][3].start()

    def recv_lat(lats, j):
        up, down, over, on = lats[j]

        @pl.when(jnp.logical_not(bottom))
        def _():
            up.wait_recv()

        @pl.when(jnp.logical_not(top))
        def _():
            down.wait_recv()

        @pl.when(top)
        def _():
            on.wait_recv()

    def sent_lat(lats):
        for up, down, over, on in lats:
            @pl.when(jnp.logical_not(top))
            def _():
                up.wait_send()

            @pl.when(top)
            def _():
                over.wait_send()

            @pl.when(near)
            def _():
                on.wait_send()

            @pl.when(jnp.logical_not(bottom))
            def _():
                down.wait_send()

    def ghost_in(buf):
        return lambda e: buf.at[:, 4 * e:4 * e + 4, :]

    lat_depth = along_lat(0, dep.at[0:1, :], dep.at[rows - 1:rows, :], lambda e: gd.at[e], hd, [(0, 1)])
    lat_1 = along_lat(4, x.at[:, :, 0, :], x.at[:, :, rows - 1, :], ghost_in(g1), h1, parts)
    lat_2 = along_lat(4 + 4 * PARTS, xe.at[:, 0:4, :], xe.at[:, 4:8, :], ghost_in(g2), h2, parts)
    start_lat(lat_depth)
    start_lat(lat_1)

    zero = jnp.zeros((8, 128), F32)

    def collect(acc, i, j, value, k):
        v = pltpu.roll(value, k + 1, 1)
        acc[i] = jnp.where(lane == k + 1, v, acc[i])
        acc[j] = jnp.where(lane == k, v, acc[j])

    def collected(acc):
        n = len(acc) // 2
        return [pltpu.roll(v, 127, 1) if i < n else v for i, v in enumerate(acc)]

    def pack(st, waits):
        def body(k, acc):
            acc = list(acc)
            for ch in range(4):
                for h in range(half):
                    i = ch * half + h
                    collect(acc, i, 4 * half + i, st[k, ch, pl.ds(PAD + 8 * h, 8), :], k)
            return tuple(acc)

        acc = (zero,) * (8 * half)
        for j, (at, n) in enumerate(parts):
            waits[j].wait()
            acc = lax.fori_loop(at, at + n, body, acc, unroll=15)
        acc = collected(acc)
        for h in range(half):
            d = dpad[pl.ds(PAD + 8 * h, 8), :].astype(F32)
            acc[h] = jnp.where(lane == nz, pltpu.roll(d, nz, 1), acc[h])
            i = 4 * half + h
            acc[i] = jnp.where(lane == nz, pltpu.roll(d, nz + 1, 1), acc[i])
        return acc

    def lon_copies(step):
        def copy(src, dst, i, device):
            return pltpu.make_async_remote_copy(src, dst, csem.at[2 * step + i], crsem.at[2 * step + i], device_id=device, device_id_type=MESH)

        return [copy(cw.at[step], he.at[step], 0, west), copy(ce.at[step], hw.at[step], 1, east)]

    def send_lon(step, acc, ends):
        for ch in range(4):
            for h in range(half):
                i = ch * half + h
                cw[step, ch, pl.ds(8 * h, 8), :] = acc[i]
                ce[step, ch, pl.ds(8 * h, 8), :] = acc[4 * half + i]
        for buf, end in zip((cw, ce), ends):
            for ch in range(4):
                buf[step, ch, 0:1, :] = end[ch:ch + 1]
                buf[step, ch, rows - 1:rows, :] = end[4 + ch:5 + ch]
        copies = lon_copies(step)
        for one in copies:
            one.start()
        return copies

    loads[0].wait()
    dpad[0:PAD, :] = jnp.zeros((8, 128), jnp.int32)
    dpad[PAD + rows:PAD + rows + 8, :] = jnp.zeros((8, 128), jnp.int32)
    lon_1 = send_lon(0, pack(st1, body_loads), [])

    @pl.when(bottom)
    def _():
        gd[0] = jnp.zeros_like(gd[0])

        def clear(k, c):
            g1[k, 0:4] = zero[0:4]
            g2[k, 0:4] = zero[0:4]
            return c

        lax.fori_loop(0, nz, clear, 0, unroll=5)

    def clear_pads(k, c):
        for ch in range(4):
            for st in (st1, st2):
                st[k, ch, 0:PAD, :] = zero
                st[k, ch, PAD + rows:PAD + rows + 8, :] = zero
        return c

    lax.fori_loop(0, nz, clear_pads, 0, unroll=5)

    first, final = lane == 0, lane == 127

    def depth_maps():
        for h in range(half):
            at = pl.ds(8 * h, 8)
            d = dpad[pl.ds(PAD + 8 * h, 8), :]
            dm[0, at, :] = d
            dm[1, at, :] = jnp.where(final, 0, pltpu.roll(d, 127, 1))
            dm[2, at, :] = jnp.where(first, 0, pltpu.roll(d, 1, 1))
            dm[3, at, :] = dpad[pl.ds(PAD + 8 * h + 1, 8), :]
            dm[4, at, :] = dpad[pl.ds(PAD + 8 * h - 1, 8), :]

    total = F32(rows * nlat)

    def rotation(h):
        row = (sub + (8 * h + lat * rows)).astype(F32)
        return 0.1 + 0.4 * (row + 0.5) / total

    def dense(warm, salt, wet):
        return jnp.where(wet, 0.075 * salt - 0.025 * warm, 0.0)

    def stencil(st, make_table, lats):
        turns = [rotation(h) for h in range(half)]

        def body(k, carry):
            grad_e = list(carry[0:half])
            grad_n = list(carry[half:2 * half])
            upper = carry[2 * half]
            if make_table:
                pivot = jnp.where(k == 0, 1.0 + MIX, 1.0 + 2.0 * MIX - MIX * upper)
                inv = 1.0 / pivot
                upper = MIX * inv
                tab[0, k] = inv
                tab[1, k] = 1.0 / (pivot - MIX)
                tab[2, k] = upper
            for h in range(half):
                at = pl.ds(8 * h, 8)
                wet = [None] + [k < dm[i, at, :] for i in range(1, 5)]
                w15 = [jnp.where(m, F32(SPR), F32(0.0)) for m in wet[1:]]
                q = [st[k, ch, pl.ds(PAD + 8 * h, 8), :] for ch in range(4)]
                qe = [pltpu.roll(v, 127, 1) for v in q]
                qw = [pltpu.roll(v, 1, 1) for v in q]
                qn = [st[k, ch, pl.ds(PAD + 8 * h + 1, 8), :] for ch in range(4)]
                qs = [st[k, ch, pl.ds(PAD + 8 * h - 1, 8), :] for ch in range(4)]
                a_e = jnp.where(final, 0.0, w15[0] - ADV * qe[2])
                a_w = jnp.where(first, 0.0, w15[1] + ADV * qw[2])
                a_n = w15[2] - ADV * qn[3]
                a_s = w15[3] + ADV * qs[3]
                centre = 1.0 - (w15[0] + w15[1]) - (w15[2] + w15[3])
                grad_e[h] = grad_e[h] + (dense(qe[0], qe[1], wet[1]) - dense(qw[0], qw[1], wet[2]))
                grad_n[h] = grad_n[h] + (dense(qn[0], qn[1], wet[3]) - dense(qs[0], qs[1], wet[4]))
                turn = turns[h]
                for ch in range(4):
                    p = (centre * q[ch] + a_e * qe[ch]) + (a_w * qw[ch] + a_n * qn[ch]) + a_s * qs[ch]
                    if ch == 2:
                        p = p + (turn * q[3] - grad_e[h])
                    if ch == 3:
                        p = p - (turn * q[2] + grad_n[h])
                    pb[k, ch, at, :] = p
            return tuple(grad_e + grad_n + [upper])

        carry = (zero,) * (2 * half + 1)
        for j, (at, n) in enumerate(parts):
            carry = lax.fori_loop(at, at + n, body, carry, unroll=5)
            relay(lats, j)
        copies = [pltpu.make_async_copy(pb.at[:, :, 0, :], pe.at[:, 0:4, :], dsem.at[0]),
                  pltpu.make_async_copy(pb.at[:, :, rows - 1, :], pe.at[:, 4:8, :], dsem.at[1])]
        for one in copies:
            one.start()
        return copies

    def columns(step):
        for h in range(half):
            at = pl.ds(8 * h, 8)
            adds = []
            for halo, own, way in ((hw, cw, 1.0), (he, ce, -1.0)):
                deep = jnp.broadcast_to(halo[0, 0, at, nz:nz + 1], (8, 128)).astype(jnp.int32)
                wet = lane < deep
                w15 = jnp.where(wet, F32(SPR), F32(0.0))
                q = [halo[step, ch, at, :] for ch in range(4)]
                coef = w15 + (way * ADV) * q[2]
                push = dense(q[0], q[1], wet)
                add = [coef * q[ch] - w15 * own[step, ch, at, :] for ch in range(4)]
                adds.append(add + [way * push])
            even = lax.rem(lane, 2) == 0
            for ch in range(5):
                w, e = adds[0][ch], pltpu.roll(adds[1][ch], 127, 1)
                ca[0, ch, at, :] = jnp.where(even, w, e)
                ca[1, ch, at, :] = jnp.where(even, e, w)
        for odd in range(2):
            for ch in range(4):
                cx[odd, ch:ch + 1, :] = ca[odd, ch, 0:1, :]
                cx[odd, 4 + ch:5 + ch, :] = ca[odd, ch, rows - 1:rows, :]
            cp[odd] = jnp.where(lo, ca[odd, 4, 0:1, :], ca[odd, 4, rows - 1:rows, :])

    outer = jnp.logical_or(first, final)

    def inverse(k, depth):
        inv = jnp.where((k + 1) == depth, tab[1, k], tab[0, k])
        return jnp.where(k < depth, inv, 0.0)

    def sweeps(dst, dst_row, gather):
        def forward(k, carry):
            new = list(carry)
            back = lax.rem(128 - k, 128)
            odd = lax.rem(k, 2)
            for h in range(half):
                at = pl.ds(8 * h, 8)
                inv = inverse(k, dm[0, at, :])
                low = MIX * inv
                j = 4 * half + h
                new[j] = new[j] + pltpu.roll(ca[odd, 4, at, :], back, 1)
                for ch in range(4):
                    side = pltpu.roll(ca[odd, ch, at, :], back, 1)
                    if ch == 2:
                        side = side + new[j]
                    p = pb[k, ch, at, :] + jnp.where(outer, side, 0.0)
                    i = ch * half + h
                    new[i] = p * inv - low * new[i]
                    vf[k, ch, at, :] = new[i]
            return tuple(new)

        lax.fori_loop(0, nz, forward, (zero,) * (5 * half), unroll=15)

        def backward(j, carry):
            k = nz - 1 - j
            up = tab[2, k]
            new = list(carry)
            for ch in range(4):
                for h in range(half):
                    i = ch * half + h
                    s = vf[k, ch, pl.ds(8 * h, 8), :] - up * carry[i]
                    dst[k, ch, pl.ds(dst_row + 8 * h, 8), :] = s
                    new[i] = s
                    if gather:
                        collect(new, 4 * half + i, 8 * half + i, s, k)
            return tuple(new)

        count = (12 if gather else 4) * half
        carry = lax.fori_loop(0, nz, backward, (zero,) * count, unroll=15)
        return collected(carry[4 * half:])

    flip = jnp.logical_and(top, sub >= 4)
    index = jnp.where(flip, 127 - lane, lane)
    sign = jnp.where(jnp.logical_and(flip, lax.rem(sub, 4) >= 2), F32(-1.0), F32(1.0))
    slope = jnp.where(lo, F32(ADV), jnp.where(top, F32(ADV), F32(-ADV)))
    push = jnp.where(sub == 3, F32(1.0), jnp.where(sub == 7, F32(-1.0), F32(0.0)))

    def mirrored(v):
        return jnp.take_along_axis(v, index, axis=1)

    eastward = lax.rem(sub, 4) == 2

    def edges(ghost, centre, solved, lats, gather, into=None):
        def both(k, c):
            return mirrored(jnp.where(lo, ghost[k, c:c + 1, :], ghost[k, c + 4:c + 5, :]))

        def forward(k, carry):
            prev, grad, flank = carry
            odd, back = lax.rem(k, 2), lax.rem(128 - k, 128)
            flank = flank + pltpu.roll(cp[odd], back, 1)
            g = mirrored(ghost[k])
            warm, salt, vel = both(k, 0), both(k, 1), both(k, 3)
            wet = k < dge[...]
            w15 = jnp.where(wet, F32(SPR), 0.0)
            grad = grad + push * dense(warm, salt, wet)
            side = pltpu.roll(cx[odd], back, 1) + jnp.where(eastward, flank, 0.0)
            side = jnp.where(outer, side, 0.0)
            p = (pe[k] + side) + ((w15 + slope * vel) * (sign * g) - w15 * centre[k]) + grad
            inv = inverse(k, dce[...])
            prev = p * inv - (MIX * inv) * prev
            ve[k] = prev
            return prev, grad, flank

        carry = (zero, zero, zero)
        for j, (at, n) in enumerate(parts):
            recv_lat(lats, j)
            carry = lax.fori_loop(at, at + n, forward, carry, unroll=15)

        def backward(j, carry):
            k = nz - 1 - j
            new = list(carry)
            new[0] = ve[k] - tab[2, k] * carry[0]
            solved[k] = new[0]
            if into is not None:
                for ch in range(4):
                    into[k, ch, 0:1, :] = new[0][ch:ch + 1]
                    into[k, ch, rows - 1:rows, :] = new[0][4 + ch:5 + ch]
            if gather:
                collect(new, 1, 2, new[0], k)
            return tuple(new)

        carry = lax.fori_loop(0, nz, backward, (zero,) * (3 if gather else 1), unroll=25)
        return collected(carry[1:])

    depth_maps()
    relay(lat_depth, 0)
    copies = stencil(st1, True, lat_1)
    for one in lon_1:
        one.wait_recv()
    columns(0)
    for one in copies + loads[1:3]:
        one.wait()
    recv_lat(lat_depth, 0)
    dce[...] = jnp.where(lo, dm[0, 0:1, :], dm[0, rows - 1:rows, :])
    dge[...] = mirrored(jnp.where(lo, gd[0], gd[1]).astype(F32)).astype(jnp.int32)
    ends = edges(g1, xc, xe, lat_1, True)
    start_lat(lat_2)
    lon_2 = send_lon(1, sweeps(st2, PAD, True), ends)
    patch = [pltpu.make_async_copy(xe.at[:, 0:4, :], st2.at[:, :, PAD, :], bsem.at[0]),
             pltpu.make_async_copy(xe.at[:, 4:8, :], st2.at[:, :, PAD + rows - 1, :], bsem.at[1])]
    for one in patch:
        one.start()
    for one in patch:
        one.wait()
    copies = stencil(st2, False, lat_2)
    for one in lon_2:
        one.wait_recv()
    columns(1)
    sweeps(out, 0, False)
    for one in copies:
        one.wait()
    edges(g2, xe, xe2, lat_2, False, out)
    for one in lon_1 + lon_2:
        one.wait_send()
    sent_lat(lat_depth)
    sent_lat(lat_1)
    sent_lat(lat_2)


def solution(mesh):
    nlon, nlat = mesh.shape["lon"], mesh.shape["lat"]

    def on_device(state, depth_levels):
        nz, _, rows, cols = state.shape
        edge = pltpu.VMEM((nz, 8, cols), F32)
        dma = pltpu.SemaphoreType.DMA
        return pl.pallas_call(
            functools.partial(kernel, nlon, nlat, nz),
            out_shape=jax.ShapeDtypeStruct(state.shape, F32),
            in_specs=[pl.BlockSpec(memory_space=pltpu.HBM)] * 2,
            out_specs=pl.BlockSpec(memory_space=pltpu.VMEM),
            scratch_shapes=[
                pltpu.VMEM((nz, 4, rows + 16, cols), F32),
                pltpu.VMEM((nz, 4, rows + 16, cols), F32),
                pltpu.VMEM((nz, 4, rows, cols), F32),
                pltpu.VMEM((nz, 4, rows, cols), F32),
                pltpu.VMEM((rows + 16, cols), jnp.int32),
                pltpu.VMEM((5, rows, cols), jnp.int32),
                pltpu.VMEM((3, nz, 8, cols), F32),
                edge, edge, edge, edge, edge, edge, edge,
                pltpu.VMEM((nz, 4, cols), F32),
                pltpu.VMEM((nz, 4, cols), F32),
                pltpu.VMEM((1, cols), jnp.int32),
                pltpu.VMEM((2, 1, cols), jnp.int32),
                pltpu.VMEM((8, cols), jnp.int32),
                pltpu.VMEM((8, cols), jnp.int32),
                pltpu.VMEM((2, 4, rows, cols), F32),
                pltpu.VMEM((2, 4, rows, cols), F32),
                pltpu.VMEM((2, 4, rows, cols), F32),
                pltpu.VMEM((2, 4, rows, cols), F32),
                pltpu.VMEM((2, 5, rows, cols), F32),
                pltpu.VMEM((2, 8, cols), F32),
                pltpu.VMEM((2, 8, cols), F32),
                dma((3 + PARTS,)), dma((4 + 8 * PARTS,)), dma((4 + 8 * PARTS,)), dma((4,)), dma((4,)), dma((2,)), dma((2,)),
            ],
            compiler_params=pltpu.CompilerParams(
                collective_id=0, has_side_effects=True, vmem_limit_bytes=50 << 20
            ),
        )(state, pltpu.with_memory_space_constraint(depth_levels, pltpu.HBM))

    return jax.shard_map(
        on_device,
        mesh=mesh,
        in_specs=(P(None, None, "lat", "lon"), P("lat", "lon")),
        out_specs=P(None, None, "lat", "lon"),
        check_vma=False,
    )
```
